32 devices in a mesh: gx: 4 (over z), gy: 4 (over y, x), gz: 2 (over core).
Axes of the slice: x: 2, y: 2, z: 4, core: 2. Of those that a mesh axis runs over, the one named last changes fastest.
Arguments:
- features: bfloat16 [4, 4, 2, 2048, 128], P('gx', 'gy', 'gz'), may hold values from -6 to 6
- positions: float32 [4, 4, 2, 3, 2048], P('gx', 'gy', 'gz'), may hold values from 0 to 1
- counts: int32 [4, 4, 2], P('gx', 'gy', 'gz'), may hold values from 1024 to 2048, as said below
- kvec: int32 [3, 1024], replicated, may hold values from -8 to 8, as said below
- sigma: float32 [128], replicated, may hold values from 0.0005 to 0.01
- w_mix: float32 [128, 128], replicated, may hold values from -0.5 to 0.5
- neighbours: int32 [4, 4, 2, 32, 2048], P('gx', 'gy', 'gz'), may hold values from 0 to 3583
- edge_weight: bfloat16 [4, 4, 2, 32, 2048], P('gx', 'gy', 'gz'), may hold values from 0.19921875 to 1
- send_list: int32 [4, 4, 2, 6, 256], P('gx', 'gy', 'gz'), may hold values from 0 to 2047
- w_message: bfloat16 [128, 128], replicated, may hold values from -0.5 to 0.5
Outputs:
- updated: bfloat16 [4, 4, 2, 2048, 128], P('gx', 'gy', 'gz')
- long_range: float32 [4, 4, 2, 2048, 128], P('gx', 'gy', 'gz')
The draws below stay inside these ranges and needn't reach their ends.
Inputs may be any that keep to these rules, and one draw needn't show every extreme that they name: `kvec`: no k-vector is zero; some component reaches each end of the range. `counts`: some domain is full and some holds 1024 atoms.
All inputs are finite; a program needn't handle non-finite values.
Results may differ from the reference program's by a relative error of at most 0.0053.
Values may be sent and summed in bfloat16 or wider, within the bound.
No kernel may reach another device: no remote copies, remote signals or barrier semaphores. Data moves between devices by JAX's collectives and lax.ppermute only.
A program may use at most 64 MiB of HBM per device.

```python
import math
import jax
import jax.numpy as jnp
from jax import lax

ATOMS = 2048
C = 128
KV = 1024
NBR = 32
BND = 256
KMAX = 8
N_GX = 4
N_GY = 4
N_GZ = 2


def draw_kvec(key, part):
    triple = jax.random.randint(key, (3, KV), -KMAX, KMAX + 1)
    empty = jnp.all(triple == 0, axis=0)
    triple = triple.at[0].set(jnp.where(empty, 1, triple[0]))
    triple = triple.at[:, 0].set(jnp.array([KMAX, -KMAX, 1], dtype=jnp.int32))
    return triple.astype(jnp.int32)


def draw_counts(key, part):
    filled = jax.random.randint(key, (N_GX, N_GY, N_GZ), ATOMS // 2, ATOMS + 1)
    filled = filled.at[0, 0, 0].set(ATOMS)
    filled = filled.at[N_GX - 1, N_GY - 1, N_GZ - 1].set(ATOMS // 2)
    return filled.astype(jnp.int32)


def plant(values, own_key, smallest, top_value):
    spot = [jax.random.randint(jax.random.fold_in(own_key, axis), (), 0, length) for axis, length in enumerate(values.shape)]
    main_axis = values.shape.index(max(values.shape))
    beside = spot[:main_axis] + [(spot[main_axis] + 1) % values.shape[main_axis]] + spot[main_axis + 1:]
    return values.at[tuple(spot)].set(smallest).at[tuple(beside)].set(top_value)


def steps_of(stream_key, shape, pieces, least, largest):
    gain = 1.0
    for dim, parts in pieces:
        steps = jax.random.uniform(jax.random.fold_in(jax.random.fold_in(stream_key, 6), dim), (parts,), jnp.float32, least / len(pieces), largest / len(pieces))
        gain = gain * jnp.repeat(jnp.exp(steps), shape[dim] // parts).reshape((-1,) + (1,) * (len(shape) - 1 - dim))
    return gain


def centred(own_key, extent, deviation, bound, split=(), held_as=jnp.bfloat16):
    values = deviation * jax.random.normal(own_key, extent, jnp.float32)
    if split:
        values = values * steps_of(own_key, extent, split, -0.22, 0.18)
    return jnp.clip(values, -bound, bound).astype(held_as)


def setup_inputs(seed: int = 0) -> dict:
    seeds = jax.random.split(jax.random.key(seed), 11)
    features = centred(seeds[0], (N_GX, N_GY, N_GZ, ATOMS, C), 1.0, 6.0, ((0, 4), (1, 4), (2, 2)))
    positions = jnp.clip(1.0 * jax.random.uniform(seeds[1], (N_GX, N_GY, N_GZ, 3, ATOMS), jnp.float32) ** steps_of(seeds[1], (N_GX, N_GY, N_GZ, 3, ATOMS), ((0, 4), (1, 4), (2, 2)), -0.2, 0.2), 0.0, 1.0)
    counts = draw_counts(jax.random.fold_in(seeds[10], 71), 0)
    kvec = draw_kvec(jax.random.fold_in(seeds[10], 71), 0)
    sigma = jnp.clip(jnp.exp(jax.random.uniform(seeds[4], (C,), jnp.float32, math.log(0.0005), math.log(0.01))), 0.0005, 0.01)
    w_mix = centred(seeds[5], (C, C), C ** -0.5, 0.5, (), jnp.float32)
    neighbours = plant(jax.random.randint(seeds[6], (N_GX, N_GY, N_GZ, NBR, ATOMS), 0, ATOMS + 6 * BND), jax.random.fold_in(seeds[6], 1), 0, (ATOMS + 6 * BND) - 1).astype(jnp.int32)
    edge_weight = jnp.clip(0.19921875 + 0.80078125 * jax.random.uniform(seeds[7], (N_GX, N_GY, N_GZ, NBR, ATOMS), jnp.float32) ** steps_of(seeds[7], (N_GX, N_GY, N_GZ, NBR, ATOMS), ((0, 4), (1, 4), (2, 2)), -0.2, 0.2), 0.19921875, 1.0).astype(jnp.bfloat16)
    send_list = plant(jax.random.randint(seeds[8], (N_GX, N_GY, N_GZ, 6, BND), 0, ATOMS), jax.random.fold_in(seeds[8], 1), 0, ATOMS - 1).astype(jnp.int32)
    w_message = centred(seeds[9], (C, C), C ** -0.5, 0.5)
    return {"features": features, "positions": positions, "counts": counts, "kvec": kvec, "sigma": sigma, "w_mix": w_mix, "neighbours": neighbours, "edge_weight": edge_weight, "send_list": send_list, "w_message": w_message}


def phase_tables(frac_x, frac_y, frac_z, kvec_f):
    theta = 2.0 * math.pi * (frac_x[:, None] * kvec_f[0][None, :] + frac_y[:, None] * kvec_f[1][None, :] + frac_z[:, None] * kvec_f[2][None, :])
    return (jnp.cos(theta).astype(jnp.bfloat16), jnp.sin(theta).astype(jnp.bfloat16))

def reference(features, positions, counts, kvec, sigma, w_mix, neighbours, edge_weight, send_list, w_message):
    domains = N_GX * N_GY * N_GZ
    feats = features.reshape(domains, ATOMS, C)
    alive = (jnp.arange(ATOMS, dtype=jnp.int32)[None, :] < counts.reshape(domains, 1)).astype(jnp.float32)
    own = jnp.where(alive[:, :, None] > 0.5, feats, jnp.zeros_like(feats))
    flat = jnp.arange(domains, dtype=jnp.int32)
    cell_x = (flat // (N_GY * N_GZ)).astype(jnp.float32)
    cell_y = (flat // N_GZ % N_GY).astype(jnp.float32)
    cell_z = (flat % N_GZ).astype(jnp.float32)
    places = positions.reshape(domains, 3, ATOMS)
    kvec_f = kvec.astype(jnp.float32)

    def tables(place, pos_x, pos_y, pos_z):
        return phase_tables((pos_x + place[0]) / N_GX, (pos_y + place[1]) / N_GY, (pos_z + place[2]) / N_GZ, kvec_f)

    def accumulate(carry, item):
        place, pos_x, pos_y, pos_z, mine = item
        cosine, sine = tables(place, pos_x, pos_y, pos_z)
        first = carry[0] + jnp.dot(cosine.T, mine, preferred_element_type=jnp.float32)
        second = carry[1] + jnp.dot(sine.T, mine, preferred_element_type=jnp.float32)
        return ((first, second), None)
    zero = jnp.zeros((KV, C), jnp.float32)
    (sum_cos, sum_sin), _ = lax.scan(accumulate, (zero, zero), (places, cell_x, cell_y, cell_z, own))
    scale = 1.0 / math.sqrt(ATOMS * domains)
    ksq = lax.optimization_barrier(jnp.sum(kvec_f * kvec_f, axis=0))
    filt = jnp.exp(-sigma[None, :] * ksq[:, None])
    g_cos = (jnp.dot(sum_cos * scale, w_mix, precision=lax.Precision.HIGHEST) * filt).astype(jnp.bfloat16)
    g_sin = (jnp.dot(sum_sin * scale, w_mix, precision=lax.Precision.HIGHEST) * filt).astype(jnp.bfloat16)
    sent = jax.vmap(lambda mine, picks: mine[picks])(own, send_list.reshape(domains, 6, BND))
    grid = sent.reshape(N_GX, N_GY, N_GZ, 6, BND, C)
    received = jnp.stack([jnp.roll(grid[:, :, :, 0], 1, axis=0), jnp.roll(grid[:, :, :, 1], -1, axis=0), jnp.roll(grid[:, :, :, 2], 1, axis=1), jnp.roll(grid[:, :, :, 3], -1, axis=1), jnp.roll(grid[:, :, :, 4], 1, axis=2), jnp.roll(grid[:, :, :, 5], -1, axis=2)], axis=3).reshape(domains, 6 * BND, C)
    picks_all = neighbours.reshape(domains, NBR, ATOMS)
    weights_all = edge_weight.reshape(domains, NBR, ATOMS)

    def finish(item):
        place, pos_x, pos_y, pos_z, mine, living, incoming, picks, weights = item
        table = jnp.concatenate([mine, incoming], axis=0)
        gathered = table[picks].astype(jnp.float32)
        message = (lax.optimization_barrier(jnp.sum(weights.astype(jnp.float32)[:, :, None] * gathered, axis=0)) / math.sqrt(NBR)).astype(jnp.bfloat16)
        hidden = jnp.dot(message, w_message, preferred_element_type=jnp.float32)
        upd = ((mine.astype(jnp.float32) + jax.nn.silu(hidden)) * living[:, None]).astype(jnp.bfloat16)
        cosine, sine = tables(place, pos_x, pos_y, pos_z)
        back = jnp.dot(cosine, g_cos, preferred_element_type=jnp.float32) + jnp.dot(sine, g_sin, preferred_element_type=jnp.float32)
        return (upd, back * (2.0 / math.sqrt(KV)) * living[:, None])
    upd_all, long_all = lax.map(finish, (places, cell_x, cell_y, cell_z, own, alive, received, picks_all, weights_all))
    return (upd_all.reshape(N_GX, N_GY, N_GZ, ATOMS, C), long_all.reshape(N_GX, N_GY, N_GZ, ATOMS, C))
```

```python
import functools
import math

import jax
import jax.numpy as jnp
import numpy as np
from jax import lax
from jax.experimental import pallas as pl
from jax.experimental.pallas import tpu as pltpu
from jax.sharding import PartitionSpec as P

F32 = jnp.float32
BF16 = jnp.bfloat16
VMEM_LIMIT = 48 << 20


def half_turn_series():
    angle = np.cos((np.arange(400) + 0.5) * np.pi / 800)
    r = 0.5 * angle
    u = r * r
    root = math.sqrt(2.0)
    even = np.polynomial.chebyshev.Chebyshev.fit(u, root * np.cos(np.pi * r), 5, domain=[0, 0.25])
    odd = np.polynomial.chebyshev.Chebyshev.fit(u, root * np.sin(np.pi * r) / r, 4, domain=[0, 0.25])
    take = lambda fit: [float(v) for v in fit.convert(kind=np.polynomial.Polynomial).coef]
    return take(even), take(odd)


EVEN, ODD = half_turn_series()


def horner(coefs, u):
    total = coefs[-1] * u + coefs[-2]
    for coef in coefs[-3::-1]:
        total = total * u + coef
    return total


def phase_kernel(
    place_ref, count_ref, sizes, pos_ref, feat_ref, kvec_ref, table_ref, sums_ref, frac_ref, own_ref
):
    atoms, width = feat_ref.shape
    kblock = kvec_ref.shape[1]

    @pl.when(pl.program_id(0) == 0)
    def _():
        rows = []
        for axis in range(3):
            place = place_ref[axis].astype(F32)
            frac = (place + pos_ref[axis : axis + 1, :]) / sizes[axis]
            high = frac.astype(BF16).astype(F32)
            middle = (frac - high).astype(BF16).astype(F32)
            rows += [high, middle, frac - high - middle]
        stacked = jnp.concatenate(rows + [jnp.zeros((16 - len(rows), atoms), F32)], axis=0)
        frac_ref[...] = stacked.T.astype(BF16)
        atom = lax.broadcasted_iota(jnp.int32, (atoms, width), 0)
        own = jnp.where(atom < count_ref[0], feat_ref[...].astype(F32), 0.0)
        own_ref[...] = own.T.astype(BF16)

    kvec = kvec_ref[...].astype(F32)
    weights = jnp.concatenate(
        [kvec[axis : axis + 1, :] for axis in range(3) for _ in range(3)]
        + [jnp.zeros((7, kblock), F32)],
        axis=0,
    ).astype(BF16)
    chunk = min(256, atoms)

    def turn(number, carry):
        rows = pl.ds(pl.multiple_of(number * chunk, chunk), chunk)
        theta = jnp.dot(frac_ref[rows, :], weights, preferred_element_type=F32)
        r = theta - jnp.round(theta)
        u = r * r
        even = horner(EVEN, u)
        odd = horner(ODD, u) * r
        table_ref[rows, :kblock] = (1.0 - odd * odd).astype(BF16)
        table_ref[rows, kblock:] = (even * odd).astype(BF16)
        return carry

    lax.fori_loop(0, atoms // chunk, turn, 0)
    sums = jnp.dot(own_ref[...], table_ref[...], preferred_element_type=F32)
    sums_ref[...] = sums.T


def phases(place, count, sizes, pos, feats, kvec):
    atoms, width = feats.shape
    kcount = kvec.shape[1]
    kblock = 128
    whole = lambda *shape: pl.BlockSpec(shape, lambda b: (0,) * len(shape))
    smem = pl.BlockSpec(memory_space=pltpu.SMEM)

    def body(place_ref, count_ref, *refs):
        phase_kernel(place_ref, count_ref, sizes, *refs)

    return pl.pallas_call(
        body,
        grid=(kcount // kblock,),
        in_specs=[
            smem,
            smem,
            whole(3, atoms),
            whole(atoms, width),
            pl.BlockSpec((3, kblock), lambda b: (0, b)),
        ],
        out_specs=[
            pl.BlockSpec((atoms, 2 * kblock), lambda b: (0, b)),
            pl.BlockSpec((2 * kblock, width), lambda b: (b, 0)),
        ],
        out_shape=[
            jax.ShapeDtypeStruct((atoms, 2 * kcount), BF16),
            jax.ShapeDtypeStruct((2 * kcount, width), F32),
        ],
        scratch_shapes=[pltpu.VMEM((atoms, 16), BF16), pltpu.VMEM((width, atoms), BF16)],
        compiler_params=pltpu.CompilerParams(vmem_limit_bytes=VMEM_LIMIT),
        name="phases",
    )(place, count, pos, feats, kvec)


def message_kernel(
    low,
    count_ref,
    nbr_ref,
    weight_ref,
    feat_ref,
    *refs,
):
    halo_refs = refs[:6]
    wmsg_ref, out_ref, high_key, low_key, edge, table_ref, adj_ref, msg_ref = refs[6:]
    slots, atoms = nbr_ref.shape
    width = feat_ref.shape[1]
    lanes = 8 * slots
    groups = atoms // 8
    span = adj_ref.shape[0] // 8
    highs = table_ref.shape[0] // low
    step = pl.program_id(0)

    @pl.when(step == 0)
    def _():
        picks = jnp.concatenate([nbr_ref[:, i * groups : (i + 1) * groups] for i in range(8)], axis=0)
        picks = picks.astype(F32).T
        upper = jnp.floor(picks * (1.0 / low))
        lane = lax.broadcasted_iota(jnp.int32, (groups, lanes), 1)
        high_key[...] = upper * 8.0 + (lane // slots).astype(F32)
        low_key[...] = picks - upper * low
        edge[...] = jnp.concatenate(
            [weight_ref[:, i * groups : (i + 1) * groups].astype(F32) for i in range(8)], axis=0
        ).T
        atom = lax.broadcasted_iota(jnp.int32, (atoms, width), 0)
        table_ref[:atoms, :] = jnp.where(atom < count_ref[0], feat_ref[...].astype(F32), 0.0).astype(BF16)
        for face, halo in enumerate(halo_refs):
            rows = halo.shape[0]
            table_ref[atoms + face * rows : atoms + (face + 1) * rows, :] = halo[...]

    high_iota = lax.broadcasted_iota(jnp.int32, (highs * 8, lanes), 0).astype(F32).astype(BF16)
    low_iota = lax.broadcasted_iota(jnp.int32, (low, lanes), 0).astype(F32).astype(BF16)

    def group(number):
        row = pl.ds(number, 1)
        high = jnp.broadcast_to(high_key[row, :], (16, lanes)).astype(BF16)
        lower = jnp.broadcast_to(low_key[row, :], (16, lanes)).astype(BF16)
        value = jnp.broadcast_to(edge[row, :], (16, lanes)).astype(BF16)
        tile = lambda x, n: jnp.concatenate([x] * (n // 16), axis=0)
        zero = jnp.zeros((), BF16)
        left = jnp.where(tile(high, highs * 8) == high_iota, tile(value, highs * 8), zero)
        right = jnp.where(tile(lower, low) == low_iota, jnp.ones((), BF16), zero)
        return lax.dot_general(left, right, (((1,), (1,)), ((), ())), preferred_element_type=F32)

    def pair(number, carry):
        first = group(step * span + 2 * number)
        second = group(step * span + 2 * number + 1)
        rows = pl.ds(pl.multiple_of(number * 16, 16), 16)
        for upper in range(highs):
            here = slice(upper * 8, upper * 8 + 8)
            block = jnp.concatenate([first[here], second[here]], axis=0).astype(BF16)
            adj_ref[rows, upper * low : (upper + 1) * low] = block
        return carry

    lax.fori_loop(0, span // 2, pair, 0, unroll=2)
    summed = jnp.dot(adj_ref[...], table_ref[...], preferred_element_type=F32)
    message = (summed / math.sqrt(slots)).astype(BF16)
    hidden = jnp.dot(message, wmsg_ref[...], preferred_element_type=F32)
    msg_ref[...] = hidden / (1.0 + jnp.exp(-hidden))
    for i in range(8):
        start = pl.multiple_of(i * groups + step * span, span)
        own = table_ref[pl.ds(start, span), :].astype(F32)
        gate = msg_ref[pl.ds(i, span, stride=8), :]
        atom = lax.broadcasted_iota(jnp.int32, (span, width), 0) + start
        out_ref[i] = jnp.where(atom < count_ref[0], own + gate, 0.0).astype(BF16)


def messages(count, nbr, weights, feats, halos, wmsg):
    slots, atoms = nbr.shape
    width = feats.shape[1]
    groups = atoms // 8
    rows = atoms + sum(halo.shape[0] for halo in halos)
    low = 256
    span = min(32, groups)
    whole = lambda *shape: pl.BlockSpec(shape, lambda b: (0,) * len(shape))
    out = pl.pallas_call(
        functools.partial(message_kernel, low),
        grid=(groups // span,),
        in_specs=[
            pl.BlockSpec(memory_space=pltpu.SMEM),
            whole(slots, atoms),
            whole(slots, atoms),
            whole(atoms, width),
            *[whole(*halo.shape) for halo in halos],
            whole(width, width),
        ],
        out_specs=pl.BlockSpec((8, span, width), lambda b: (0, b, 0)),
        out_shape=jax.ShapeDtypeStruct((8, groups, width), BF16),
        scratch_shapes=[
            pltpu.VMEM((groups, 8 * slots), F32),
            pltpu.VMEM((groups, 8 * slots), F32),
            pltpu.VMEM((groups, 8 * slots), F32),
            pltpu.VMEM((rows, width), BF16),
            pltpu.VMEM((8 * span, rows), BF16),
            pltpu.VMEM((8 * span, width), F32),
        ],
        compiler_params=pltpu.CompilerParams(vmem_limit_bytes=VMEM_LIMIT),
        name="messages",
    )(count, nbr, weights, feats, *halos, wmsg)
    return out.reshape(atoms, width)


def back_kernel(scale, count_ref, table_ref, g_ref, out_ref):
    rows, width = out_ref.shape
    back = jnp.dot(table_ref[...], g_ref[...], preferred_element_type=F32)
    atom = lax.broadcasted_iota(jnp.int32, (rows, width), 0) + pl.program_id(0) * rows
    out_ref[...] = jnp.where(atom < count_ref[0], back * scale, 0.0)


def back(count, table, g, scale):
    atoms, depth = table.shape
    width = g.shape[1]
    block = min(512, atoms)
    return pl.pallas_call(
        functools.partial(back_kernel, scale),
        grid=(atoms // block,),
        in_specs=[
            pl.BlockSpec(memory_space=pltpu.SMEM),
            pl.BlockSpec((block, depth), lambda b: (b, 0)),
            pl.BlockSpec((depth, width), lambda b: (0, 0)),
        ],
        out_specs=pl.BlockSpec((block, width), lambda b: (b, 0)),
        out_shape=jax.ShapeDtypeStruct((atoms, width), F32),
        compiler_params=pltpu.CompilerParams(vmem_limit_bytes=VMEM_LIMIT),
        name="back",
    )(count, table, g)


def passed_along(value, axis, steps):
    size = lax.axis_size(axis)
    pairs = [(source, (source + steps) % size) for source in range(size)]
    return lax.ppermute(value, axis, pairs)


def filtered(sums, ksq, sigma, w_mix):
    mixed = jnp.dot(sums, w_mix, precision=lax.Precision.HIGHEST)
    return (mixed * jnp.exp(-sigma[None, :] * ksq[:, None])).astype(BF16)


def reduced_and_filtered(sums, ksq, sigma, w_mix, scale):
    size_z = lax.axis_size("gz")
    plane = lax.axis_size("gx") * lax.axis_size("gy")
    rows, width = sums.shape
    part = rows // (size_z * plane)
    here_z = lax.axis_index("gz")
    here_xy = lax.axis_index("gx") * lax.axis_size("gy") + lax.axis_index("gy")
    sums = lax.all_to_all(sums, "gz", 0, 0, tiled=True)
    sums = jnp.sum(sums.reshape(size_z, rows // size_z, width), axis=0)
    sums = lax.all_to_all(sums, ("gx", "gy"), 0, 0, tiled=True)
    sums = jnp.sum(sums.reshape(plane, part, width), axis=0)
    mine = lax.dynamic_slice_in_dim(ksq, (here_z * plane + here_xy) * part, part)
    g = filtered(sums * scale, mine, sigma, w_mix)
    g = jnp.broadcast_to(g[None], (plane, part, width))
    g = lax.all_to_all(g, ("gx", "gy"), 0, 0, tiled=True).reshape(plane * part, width)
    g = jnp.broadcast_to(g[None], (size_z, plane * part, width))
    return lax.all_to_all(g, "gz", 0, 0, tiled=True).reshape(rows, width)


def shards(
    features, positions, counts, kvec, sigma, w_mix, neighbours, edge_weight, send_list, w_message
):
    atoms = features.shape[3]
    width = features.shape[4]
    kcount = kvec.shape[1]
    slots = neighbours.shape[3]
    feats = features.reshape(atoms, width)
    count = counts.reshape(1)
    sizes = [lax.axis_size(axis) for axis in ("gx", "gy", "gz")]
    devices = sizes[0] * sizes[1] * sizes[2]
    place = jnp.stack([lax.axis_index(axis) for axis in ("gx", "gy", "gz")]).astype(jnp.int32)

    alive = jnp.arange(atoms, dtype=jnp.int32) < count[0]
    own = jnp.where(alive[:, None], feats, jnp.zeros_like(feats))
    selector = (
        send_list.reshape(-1)[:, None] == jnp.arange(atoms, dtype=jnp.int32)[None, :]
    ).astype(BF16)
    outgoing = jnp.dot(selector, own, preferred_element_type=F32).astype(BF16)
    outgoing = outgoing.reshape(6, -1, width)
    halos = [
        passed_along(outgoing[2 * number + side], axis, 1 - 2 * side)
        for number, axis in enumerate(("gx", "gy", "gz"))
        for side in range(2)
    ]

    table, sums = phases(place, count, sizes, positions.reshape(3, atoms), feats, kvec)
    kvec_f = kvec.astype(F32)
    ksq = jnp.sum(kvec_f * kvec_f, axis=0).reshape(-1, 1, 128)
    ksq = jnp.broadcast_to(ksq, (kcount // 128, 2, 128)).reshape(2 * kcount)
    g = reduced_and_filtered(sums, ksq, sigma, w_mix, 1.0 / math.sqrt(atoms * devices))
    updated = messages(
        count, neighbours.reshape(slots, atoms), edge_weight.reshape(slots, atoms), feats, halos, w_message
    )
    long_range = back(count, table, g, 2.0 / math.sqrt(kcount))
    return (updated.reshape(1, 1, 1, atoms, width), long_range.reshape(1, 1, 1, atoms, width))


def solution(mesh):
    split = P("gx", "gy", "gz", None, None)
    placed = (split, split, P("gx", "gy", "gz"), P(), P(), P(), split, split, split, P())
    return jax.shard_map(
        shards, mesh=mesh, in_specs=placed, out_specs=(split, split), check_vma=False
    )
```

```python
import functools
import math

import jax
import jax.numpy as jnp
import numpy as np
from jax import lax
from jax.experimental import pallas as pl
from jax.experimental.pallas import tpu as pltpu
from jax.sharding import PartitionSpec as P

F32 = jnp.float32
BF16 = jnp.bfloat16
VMEM_LIMIT = 14 << 20


def half_turn_series():
    angle = np.cos((np.arange(400) + 0.5) * np.pi / 800)
    r = 0.5 * angle
    u = r * r
    root = math.sqrt(2.0)
    even = np.polynomial.chebyshev.Chebyshev.fit(u, root * np.cos(np.pi * r), 4, domain=[0, 0.25])
    odd = np.polynomial.chebyshev.Chebyshev.fit(u, root * np.sin(np.pi * r) / r, 3, domain=[0, 0.25])
    take = lambda fit: [float(v) for v in fit.convert(kind=np.polynomial.Polynomial).coef]
    return take(even), take(odd)


EVEN, ODD = half_turn_series()


def in_hbm(*values):
    return [pltpu.with_memory_space_constraint(value, pltpu.HBM) for value in values]


def horner(coefs, u):
    total = coefs[-1] * u + coefs[-2]
    for coef in coefs[-3::-1]:
        total = total * u + coef
    return total


def phase_kernel(
    sizes,
    scale,
    paired,
    place_ref,
    count_ref,
    pos_ref,
    feat_ref,
    kvec_ref,
    sigma_ref,
    mix_ref,
    table_ref,
    *refs,
):
    out_refs = refs[: 1 + paired]
    frac_ref, own_ref, mix_turned, decay_ref = refs[1 + paired :]
    atoms, width = feat_ref.shape
    kblock = kvec_ref.shape[1]
    step = pl.program_id(0)

    @pl.when(step == 0)
    def _():
        rows = []
        for axis in range(3):
            frac = (place_ref[axis].astype(F32) + pos_ref[axis]) / sizes[axis]
            high = frac.astype(BF16).astype(F32)
            middle = (frac - high).astype(BF16).astype(F32)
            rows += [high, middle, frac - high - middle]
        stacked = jnp.concatenate(rows + [jnp.zeros((16 - len(rows), atoms), F32)], axis=0)
        frac_ref[...] = stacked.T.astype(BF16)
        atom = lax.broadcasted_iota(jnp.int32, (atoms, width), 0)
        own = jnp.where(atom < count_ref[0], feat_ref[...].astype(F32), 0.0)
        own_ref[...] = own.T.astype(BF16)
        mix_turned[...] = mix_ref[...].T
        decay_ref[...] = jnp.broadcast_to(-sigma_ref[...], (width, width)).T

    kvec = kvec_ref[...].astype(F32)
    weights = jnp.concatenate(
        [kvec[axis : axis + 1, :] for axis in range(3) for _ in range(3)]
        + [jnp.zeros((7, kblock), F32)],
        axis=0,
    ).astype(BF16)
    chunk = min(256, atoms)
    for start in range(0, atoms, chunk):
        rows = slice(start, start + chunk)
        theta = jnp.dot(frac_ref[rows, :], weights, preferred_element_type=F32)
        r = theta - jnp.round(theta)
        u = r * r
        even = horner(EVEN, u)
        odd = horner(ODD, u) * r
        cosine = (1.0 - odd * odd).astype(BF16)
        sine = (even * odd).astype(BF16)
        table_ref[rows, :kblock] = cosine
        table_ref[rows, kblock:] = sine

    sums = jnp.dot(own_ref[...], table_ref[...], preferred_element_type=F32)
    ksq = jnp.sum(kvec * kvec, axis=0, keepdims=True)
    decay = jnp.exp(decay_ref[:, :1] * ksq)
    mixed = jnp.dot(
        mix_turned[...], sums * scale, precision=lax.Precision.HIGHEST, preferred_element_type=F32
    )
    result = (mixed * jnp.concatenate([decay, decay], axis=1)).T
    if paired:
        half = pl.num_programs(0) // 2

        @pl.when(step < half)
        def _():
            out_refs[0][...] = result

        @pl.when(step >= half)
        def _():
            out_refs[1][...] = result
    else:
        out_refs[0][...] = result


def phases(place, count, sizes, scale, pos, feats, kvec, sigma, w_mix):
    atoms, width = feats.shape
    kcount = kvec.shape[1]
    kblock = 256 if kcount % 512 == 0 else 128
    steps = kcount // kblock
    half = steps // 2
    paired = sizes[2] == 2
    whole = lambda *shape: pl.BlockSpec(shape, lambda b, *_: (0,) * len(shape))

    def kvec_map(b, place_ref, count_ref):
        return (0, lax.rem(b + (1 - place_ref[2]) * half, steps) if paired else b)

    if paired:
        out_specs = [
            pl.BlockSpec((2 * kblock, width), lambda b, *_: (jnp.minimum(b, half - 1), 0)),
            pl.BlockSpec((2 * kblock, width), lambda b, *_: (jnp.maximum(b - half, 0), 0)),
        ]
        out_shape = [jax.ShapeDtypeStruct((kcount, width), F32)] * 2
    else:
        out_specs = [pl.BlockSpec((2 * kblock, width), lambda b, *_: (b, 0))]
        out_shape = [jax.ShapeDtypeStruct((2 * kcount, width), F32)]
    return pl.pallas_call(
        functools.partial(phase_kernel, sizes, scale, paired),
        grid_spec=pltpu.PrefetchScalarGridSpec(
            num_scalar_prefetch=2,
            grid=(steps,),
            in_specs=[
                whole(3, 1, atoms),
                whole(atoms, width),
                pl.BlockSpec((3, kblock), kvec_map),
                whole(1, width),
                whole(width, width),
            ],
            out_specs=[pl.BlockSpec((atoms, 2 * kblock), lambda b, *_: (0, b)), *out_specs],
            scratch_shapes=[
                pltpu.VMEM((atoms, 16), BF16),
                pltpu.VMEM((width, atoms), BF16),
                pltpu.VMEM((width, width), F32),
                pltpu.VMEM((width, width), F32),
            ],
        ),
        out_shape=[pltpu.HBM((atoms, 2 * kcount), BF16), *out_shape],
        compiler_params=pltpu.CompilerParams(vmem_limit_bytes=VMEM_LIMIT),
        name="phases",
    )(place, count, *in_hbm(pos.reshape(3, 1, atoms), feats, kvec, sigma.reshape(1, width), w_mix))


def select_kernel(count_ref, send_ref, feat_ref, *refs):
    *out_refs, own_ref = refs
    faces, _, picks = send_ref.shape
    atoms, width = feat_ref.shape
    atom = lax.broadcasted_iota(jnp.int32, (atoms, width), 0)
    own_ref[...] = jnp.where(atom < count_ref[0], feat_ref[...].astype(F32), 0.0).astype(BF16)
    rows = jnp.concatenate([send_ref[face] for face in range(faces)], axis=0).astype(F32)
    columns = jnp.concatenate([rows, jnp.zeros((8 - faces, picks), F32)], axis=0).T
    chunk = min(256, atoms)
    lane = lax.broadcasted_iota(jnp.int32, (picks, chunk), 1).astype(F32).astype(BF16)
    one, zero = jnp.ones((), BF16), jnp.zeros((), BF16)
    for face in range(faces):
        spread = jnp.broadcast_to(columns[:, face : face + 1], (picks, 128))
        total = jnp.zeros((picks, width), F32)
        for start in range(0, atoms, chunk):
            key = (spread - float(start)).astype(BF16)
            hot = jnp.where(jnp.concatenate([key] * (chunk // 128), axis=1) == lane, one, zero)
            total += jnp.dot(hot, own_ref[start : start + chunk, :], preferred_element_type=F32)
        if face < 4:
            out_refs[face][...] = total.astype(BF16)
        else:
            out_refs[4][face - 4] = total.astype(BF16)


def selected(count, send, feats):
    atoms, width = feats.shape
    faces, picks = send.shape
    return pl.pallas_call(
        select_kernel,
        in_specs=[
            pl.BlockSpec(memory_space=pltpu.SMEM),
            pl.BlockSpec((faces, 1, picks), lambda: (0, 0, 0)),
            pl.BlockSpec((atoms, width), lambda: (0, 0)),
        ],
        out_specs=[pl.BlockSpec(memory_space=pltpu.VMEM)] * 5,
        out_shape=[jax.ShapeDtypeStruct((picks, width), BF16)] * 4
        + [jax.ShapeDtypeStruct((2, picks, width), BF16)],
        scratch_shapes=[pltpu.VMEM((atoms, width), BF16)],
        compiler_params=pltpu.CompilerParams(vmem_limit_bytes=VMEM_LIMIT),
        name="selected",
    )(count, *in_hbm(send.reshape(faces, 1, picks), feats))


def total_kernel(parts_ref, out_ref):
    total = parts_ref[0].astype(F32)
    for part in range(1, parts_ref.shape[0]):
        total += parts_ref[part].astype(F32)
    total = total.astype(BF16)
    for part in range(parts_ref.shape[0]):
        out_ref[part] = total


def totals(parts):
    return pl.pallas_call(
        total_kernel,
        in_specs=[pl.BlockSpec(memory_space=pltpu.VMEM)],
        out_specs=pl.BlockSpec(memory_space=pltpu.VMEM),
        out_shape=jax.ShapeDtypeStruct(parts.shape, BF16),
        compiler_params=pltpu.CompilerParams(vmem_limit_bytes=4 << 20),
        name="totals",
    )(parts)


def message_kernel(low, count_ref, nbr_ref, weight_ref, feat_ref, *refs):
    halo_refs = [*refs[:4], refs[4].at[0], refs[4].at[1]]
    wmsg_ref, out_ref, high_key, low_key, edge, table_ref, adj_ref, msg_ref = refs[5:]
    slots, atoms = nbr_ref.shape
    width = feat_ref.shape[1]
    lanes = 8 * slots
    groups = atoms // 8
    span = adj_ref.shape[0] // 8
    highs = table_ref.shape[0] // low
    step = pl.program_id(0)

    @pl.when(step == 0)
    def _():
        stack = lambda ref: jnp.concatenate(
            [ref[:, i * groups : (i + 1) * groups].astype(F32) for i in range(8)], axis=0
        )
        picks = stack(nbr_ref)
        upper = jnp.floor(picks * (1.0 / low))
        low_key[...] = picks - upper * low
        place = lax.broadcasted_iota(jnp.int32, (lanes, groups), 0) // slots
        high_key[...] = (upper * 8.0 + place.astype(F32)).T
        edge[...] = stack(weight_ref).T
        atom = lax.broadcasted_iota(jnp.int32, (atoms, width), 0)
        table_ref[:atoms, :] = jnp.where(atom < count_ref[0], feat_ref[...].astype(F32), 0.0).astype(BF16)
        for face, halo in enumerate(halo_refs):
            rows = halo.shape[0]
            table_ref[atoms + face * rows : atoms + (face + 1) * rows, :] = halo[...]

    high_iota = lax.broadcasted_iota(jnp.int32, (highs * 8, lanes), 0).astype(F32).astype(BF16)
    lane = lax.broadcasted_iota(jnp.int32, (lanes, 128), 1).astype(F32)
    low_iota = [(lane + 128.0 * part).astype(BF16) for part in range(low // 128)]
    tile = lambda x, n: jnp.concatenate([x] * (n // 16), axis=0)
    zero = jnp.zeros((), BF16)
    one = jnp.ones((), BF16)
    first_lane = pl.multiple_of((step * span) // 128 * 128, 128)
    lows = pltpu.roll(low_key[:, pl.ds(first_lane, 128)], (128 - (step * span) % 128) % 128, 1)

    def group(number):
        row = pl.ds(step * span + number, 1)
        high = jnp.broadcast_to(high_key[row, :], (16, lanes)).astype(BF16)
        value = jnp.broadcast_to(edge[row, :], (16, lanes)).astype(BF16)
        left = jnp.where(tile(high, highs * 8) == high_iota, tile(value, highs * 8), zero)
        lower = jnp.broadcast_to(lows[:, number : number + 1], (lanes, 128)).astype(BF16)
        right = jnp.concatenate([jnp.where(lower == iota, one, zero) for iota in low_iota], axis=1)
        return jnp.dot(left, right, preferred_element_type=F32)

    for number in range(0, span, 2):
        first = group(number)
        second = group(number + 1)
        for upper in range(highs):
            here = slice(upper * 8, upper * 8 + 8)
            block = jnp.concatenate([first[here], second[here]], axis=0).astype(BF16)
            adj_ref[number * 8 : number * 8 + 16, upper * low : (upper + 1) * low] = block

    summed = jnp.dot(adj_ref[...], table_ref[...], preferred_element_type=F32)
    message = (summed / math.sqrt(slots)).astype(BF16)
    hidden = jnp.dot(message, wmsg_ref[...], preferred_element_type=F32)
    msg_ref[...] = hidden / (1.0 + jnp.exp(-hidden))
    for i in range(8):
        start = pl.multiple_of(i * groups + step * span, span)
        own = table_ref[pl.ds(start, span), :].astype(F32)
        gate = msg_ref[pl.ds(i, span, stride=8), :]
        atom = lax.broadcasted_iota(jnp.int32, (span, width), 0) + start
        out_ref[i] = jnp.where(atom < count_ref[0], own + gate, 0.0).astype(BF16)


def messages(count, nbr, weights, feats, halos, wmsg):
    slots, atoms = nbr.shape
    width = feats.shape[1]
    groups = atoms // 8
    rows = atoms + 6 * halos[0].shape[0]
    low = 256
    span = min(64, groups)
    whole = lambda *shape: pl.BlockSpec(shape, lambda b: (0,) * len(shape))
    out = pl.pallas_call(
        functools.partial(message_kernel, low),
        grid=(groups // span,),
        in_specs=[
            pl.BlockSpec(memory_space=pltpu.SMEM),
            whole(slots, atoms),
            whole(slots, atoms),
            whole(atoms, width),
            *[whole(*halo.shape) for halo in halos],
            whole(width, width),
        ],
        out_specs=pl.BlockSpec((8, span, width), lambda b: (0, b, 0)),
        out_shape=jax.ShapeDtypeStruct((8, groups, width), BF16),
        scratch_shapes=[
            pltpu.VMEM((groups, 8 * slots), F32),
            pltpu.VMEM((8 * slots, groups), F32),
            pltpu.VMEM((groups, 8 * slots), F32),
            pltpu.VMEM((rows, width), BF16),
            pltpu.VMEM((8 * span, rows), BF16),
            pltpu.VMEM((8 * span, width), F32),
        ],
        compiler_params=pltpu.CompilerParams(vmem_limit_bytes=VMEM_LIMIT),
        name="messages",
    )(count, *in_hbm(nbr, weights, feats), *halos, *in_hbm(wmsg))
    return out.reshape(atoms, width)


def back_kernel(scale, count_ref, table_hbm, *refs):
    *g_refs, out_ref, table_ref, sems = refs
    atoms, width = out_ref.shape
    pieces = sems.shape[0]
    rows = atoms // pieces
    copies = []
    for piece in range(pieces):
        here = pl.ds(piece * rows, rows)
        copies.append(pltpu.make_async_copy(table_hbm.at[here], table_ref.at[here], sems.at[piece]))
        copies[-1].start()
    for piece in range(pieces):
        copies[piece].wait()
        here = slice(piece * rows, (piece + 1) * rows)
        back = jnp.zeros((rows, width), F32)
        start = 0
        for g_ref in g_refs:
            depth = g_ref.shape[0]
            back += jnp.dot(
                table_ref[here, start : start + depth], g_ref[...], preferred_element_type=F32
            )
            start += depth
        atom = lax.broadcasted_iota(jnp.int32, (rows, width), 0) + piece * rows
        out_ref[here, :] = jnp.where(atom < count_ref[0], back * scale, 0.0)


def back(count, table, gs, scale):
    atoms, depth = table.shape
    width = gs[0].shape[1]
    vmem = pl.BlockSpec(memory_space=pltpu.VMEM)
    return pl.pallas_call(
        functools.partial(back_kernel, scale),
        in_specs=[
            pl.BlockSpec(memory_space=pltpu.SMEM),
            pl.BlockSpec(memory_space=pltpu.HBM),
            *[vmem for _ in gs],
        ],
        out_specs=vmem,
        out_shape=jax.ShapeDtypeStruct((atoms, width), F32),
        scratch_shapes=[pltpu.VMEM((atoms, depth), BF16), pltpu.SemaphoreType.DMA((8,))],
        compiler_params=pltpu.CompilerParams(vmem_limit_bytes=VMEM_LIMIT),
        name="back",
    )(count, *in_hbm(table), *gs)


def passed_along(value, axis, steps):
    size = lax.axis_size(axis)
    pairs = [(source, (source + steps) % size) for source in range(size)]
    return lax.ppermute(value, axis, pairs)


def shards(
    features, positions, counts, kvec, sigma, w_mix, neighbours, edge_weight, send_list, w_message
):
    atoms = features.shape[3]
    width = features.shape[4]
    kcount = kvec.shape[1]
    slots = neighbours.shape[3]
    feats = features.reshape(atoms, width)
    count = counts.reshape(1)
    sizes = [lax.axis_size(axis) for axis in ("gx", "gy", "gz")]
    plane = sizes[0] * sizes[1]
    devices = plane * sizes[2]
    place = jnp.stack([lax.axis_index(axis) for axis in ("gx", "gy", "gz")]).astype(jnp.int32)
    paired = sizes[2] == 2

    outgoing = selected(count, send_list.reshape(6, -1), feats)
    halos = [
        passed_along(outgoing[2 * number + side], axis, 1 - 2 * side)
        for number, axis in enumerate(("gx", "gy"))
        for side in range(2)
    ]
    if paired:
        halos.append(passed_along(outgoing[4], "gz", 1))
    else:
        halos.append(jnp.stack([passed_along(outgoing[4][side], "gz", 1 - 2 * side) for side in range(2)]))
    positions, _ = lax.optimization_barrier((positions, outgoing))
    scale = 1.0 / math.sqrt(atoms * devices)
    table, *sums = phases(
        place, count, sizes, scale, positions.reshape(3, atoms), feats, kvec, sigma, w_mix
    )
    if paired:
        mine = sums[1] + passed_along(sums[0], "gz", 1)
    else:
        parts = lax.all_to_all(sums[0], "gz", 0, 0, tiled=True)
        mine = jnp.sum(parts.reshape(sizes[2], -1, width), axis=0)
    mine, halos = lax.optimization_barrier((mine, halos))
    part = mine.shape[0] // plane
    received = lax.all_to_all(mine.reshape(plane, part, width), ("gx", "gy"), 0, 0, tiled=True)

    neighbours, _ = lax.optimization_barrier((neighbours, mine))
    updated = messages(
        count, neighbours.reshape(slots, atoms), edge_weight.reshape(slots, atoms), feats, halos, w_message
    )

    received, updated = lax.optimization_barrier((received, updated))
    g = lax.all_to_all(totals(received), ("gx", "gy"), 0, 0, tiled=True).reshape(plane * part, width)
    if paired:
        gs = [passed_along(g, "gz", 1), g]
    else:
        gs = [lax.all_gather(g, "gz", tiled=True)]
    long_range = back(count, table, gs, 2.0 / math.sqrt(kcount))
    return (updated.reshape(1, 1, 1, atoms, width), long_range.reshape(1, 1, 1, atoms, width))


def solution(mesh):
    split = P("gx", "gy", "gz", None, None)
    placed = (split, split, P("gx", "gy", "gz"), P(), P(), P(), split, split, split, P())
    return jax.shard_map(
        shards, mesh=mesh, in_specs=placed, out_specs=(split, split), check_vma=False
    )
```

```python
import functools
import math

import jax
import jax.numpy as jnp
import numpy as np
from jax import lax
from jax.experimental import pallas as pl
from jax.experimental.pallas import tpu as pltpu
from jax.sharding import PartitionSpec as P

F32 = jnp.float32
BF16 = jnp.bfloat16
VMEM_LIMIT = 14 << 20
EARLY = 2


def half_turn_series():
    angle = np.cos((np.arange(400) + 0.5) * np.pi / 800)
    r = 0.5 * angle
    u = r * r
    root = math.sqrt(2.0)
    even = np.polynomial.chebyshev.Chebyshev.fit(u, root * np.cos(np.pi * r), 4, domain=[0, 0.25])
    odd = np.polynomial.chebyshev.Chebyshev.fit(u, root * np.sin(np.pi * r) / r, 4, domain=[0, 0.25])
    take = lambda fit: [float(v) for v in fit.convert(kind=np.polynomial.Polynomial).coef]
    return take(even), take(odd)


EVEN, ODD = half_turn_series()


def in_hbm(*values):
    return [pltpu.with_memory_space_constraint(value, pltpu.HBM) for value in values]


def horner(coefs, u):
    total = coefs[-1] * u + coefs[-2]
    for coef in coefs[-3::-1]:
        total = total * u + coef
    return total


def phase_kernel(
    sizes,
    scale,
    paired,
    place_ref,
    count_ref,
    pos_ref,
    feat_ref,
    kvec_ref,
    sigma_ref,
    mix_ref,
    table_ref,
    *refs,
):
    out_refs = refs[: 1 + paired]
    frac_ref, own_ref, mix_turned, decay_ref = refs[1 + paired :]
    atoms, width = feat_ref.shape
    kblock = kvec_ref.shape[1]
    step = pl.program_id(0)

    @pl.when(step == 0)
    def _():
        rows = []
        for axis in range(3):
            frac = (place_ref[axis].astype(F32) + pos_ref[axis]) / sizes[axis]
            high = frac.astype(BF16).astype(F32)
            middle = (frac - high).astype(BF16).astype(F32)
            rows += [high, middle, frac - high - middle]
        stacked = jnp.concatenate(rows + [jnp.zeros((16 - len(rows), atoms), F32)], axis=0)
        frac_ref[...] = stacked.T.astype(BF16)
        atom = lax.broadcasted_iota(jnp.int32, (atoms, width), 0)
        own = jnp.where(atom < count_ref[0], feat_ref[...].astype(F32), 0.0)
        own_ref[...] = own.T.astype(BF16)
        mix_turned[...] = mix_ref[...].T
        decay_ref[...] = jnp.broadcast_to(-sigma_ref[...], (width, width)).T

    kvec = kvec_ref[...].astype(F32)
    weights = jnp.concatenate(
        [kvec[axis : axis + 1, :] for axis in range(3) for _ in range(3)]
        + [jnp.zeros((7, kblock), F32)],
        axis=0,
    ).astype(BF16)
    chunk = min(256, atoms)
    for start in range(0, atoms, chunk):
        rows = slice(start, start + chunk)
        theta = jnp.dot(frac_ref[rows, :], weights, preferred_element_type=F32)
        r = theta - jnp.round(theta)
        u = r * r
        even = horner(EVEN, u)
        odd = horner(ODD, u) * r
        cosine = (1.0 - odd * odd).astype(BF16)
        sine = (even * odd).astype(BF16)
        table_ref[rows, :kblock] = cosine
        table_ref[rows, kblock:] = sine

    sums = jnp.dot(own_ref[...], table_ref[...], preferred_element_type=F32)
    ksq = jnp.sum(kvec * kvec, axis=0, keepdims=True)
    decay = jnp.exp(decay_ref[:, :1] * ksq)
    mixed = jnp.dot(
        mix_turned[...], sums * scale, precision=lax.Precision.HIGHEST, preferred_element_type=F32
    )
    result = (mixed * jnp.concatenate([decay, decay], axis=1)).T
    if paired:
        half = pl.num_programs(0) // 2

        @pl.when(step < half)
        def _():
            out_refs[0][...] = result

        @pl.when(step >= half)
        def _():
            out_refs[1][...] = result
    else:
        out_refs[0][...] = result


def phases(place, count, sizes, scale, pos, feats, kvec, sigma, w_mix):
    atoms, width = feats.shape
    kcount = kvec.shape[1]
    kblock = 256 if kcount % 512 == 0 else 128
    steps = kcount // kblock
    half = steps // 2
    paired = sizes[2] == 2
    whole = lambda *shape: pl.BlockSpec(shape, lambda b, *_: (0,) * len(shape))

    def kvec_map(b, place_ref, count_ref):
        return (0, lax.rem(b + (1 - place_ref[2]) * half, steps) if paired else b)

    if paired:
        out_specs = [
            pl.BlockSpec((2 * kblock, width), lambda b, *_: (jnp.minimum(b, half - 1), 0)),
            pl.BlockSpec((2 * kblock, width), lambda b, *_: (jnp.maximum(b - half, 0), 0)),
        ]
        out_shape = [jax.ShapeDtypeStruct((kcount, width), F32)] * 2
    else:
        out_specs = [pl.BlockSpec((2 * kblock, width), lambda b, *_: (b, 0))]
        out_shape = [jax.ShapeDtypeStruct((2 * kcount, width), F32)]
    return pl.pallas_call(
        functools.partial(phase_kernel, sizes, scale, paired),
        grid_spec=pltpu.PrefetchScalarGridSpec(
            num_scalar_prefetch=2,
            grid=(steps,),
            in_specs=[
                whole(3, 1, atoms),
                whole(atoms, width),
                pl.BlockSpec((3, kblock), kvec_map),
                whole(1, width),
                whole(width, width),
            ],
            out_specs=[pl.BlockSpec((atoms, 2 * kblock), lambda b, *_: (0, b)), *out_specs],
            scratch_shapes=[
                pltpu.VMEM((atoms, 16), BF16),
                pltpu.VMEM((width, atoms), BF16),
                pltpu.VMEM((width, width), F32),
                pltpu.VMEM((width, width), F32),
            ],
        ),
        out_shape=[pltpu.HBM((atoms, 2 * kcount), BF16), *out_shape],
        compiler_params=pltpu.CompilerParams(vmem_limit_bytes=VMEM_LIMIT),
        name="phases",
    )(place, count, *in_hbm(pos.reshape(3, 1, atoms), feats, kvec, sigma.reshape(1, width), w_mix))


def select_kernel(count_ref, send_ref, feat_ref, *refs):
    *out_refs, own_ref = refs
    faces, _, picks = send_ref.shape
    atoms, width = feat_ref.shape
    atom = lax.broadcasted_iota(jnp.int32, (atoms, width), 0)
    own_ref[...] = jnp.where(atom < count_ref[0], feat_ref[...].astype(F32), 0.0).astype(BF16)
    rows = jnp.concatenate([send_ref[face] for face in range(faces)], axis=0).astype(F32)
    columns = jnp.concatenate([rows, jnp.zeros((8 - faces, picks), F32)], axis=0).T
    chunk = min(256, atoms)
    lane = lax.broadcasted_iota(jnp.int32, (picks, chunk), 1).astype(F32).astype(BF16)
    one, zero = jnp.ones((), BF16), jnp.zeros((), BF16)
    for face in range(faces):
        spread = jnp.broadcast_to(columns[:, face : face + 1], (picks, 128))
        total = jnp.zeros((picks, width), F32)
        for start in range(0, atoms, chunk):
            key = (spread - float(start)).astype(BF16)
            hot = jnp.where(jnp.concatenate([key] * (chunk // 128), axis=1) == lane, one, zero)
            total += jnp.dot(hot, own_ref[start : start + chunk, :], preferred_element_type=F32)
        if face < 4:
            out_refs[face][...] = total.astype(BF16)
        else:
            out_refs[4][face - 4] = total.astype(BF16)


def selected(count, send, feats):
    atoms, width = feats.shape
    faces, _, picks = send.shape
    return pl.pallas_call(
        select_kernel,
        in_specs=[
            pl.BlockSpec(memory_space=pltpu.SMEM),
            pl.BlockSpec((faces, 1, picks), lambda: (0, 0, 0)),
            pl.BlockSpec((atoms, width), lambda: (0, 0)),
        ],
        out_specs=[pl.BlockSpec(memory_space=pltpu.VMEM)] * 6,
        out_shape=[jax.ShapeDtypeStruct((picks, width), BF16)] * 4
        + [jax.ShapeDtypeStruct((2, picks, width), BF16), jax.ShapeDtypeStruct((atoms, width), BF16)],
        compiler_params=pltpu.CompilerParams(vmem_limit_bytes=VMEM_LIMIT),
        name="selected",
    )(count, *in_hbm(send, feats))


def total_kernel(parts_ref, out_ref):
    total = parts_ref[0].astype(F32)
    for part in range(1, parts_ref.shape[0]):
        total += parts_ref[part].astype(F32)
    total = total.astype(BF16)
    for part in range(parts_ref.shape[0]):
        out_ref[part] = total


def totals(parts):
    return pl.pallas_call(
        total_kernel,
        in_specs=[pl.BlockSpec(memory_space=pltpu.VMEM)],
        out_specs=pl.BlockSpec(memory_space=pltpu.VMEM),
        out_shape=jax.ShapeDtypeStruct(parts.shape, BF16),
        compiler_params=pltpu.CompilerParams(vmem_limit_bytes=4 << 20),
        name="totals",
    )(parts)


def prepare_kernel(low, nbr_ref, weight_ref, high_key, low_key, edge):
    slots, atoms = nbr_ref.shape
    groups, lanes = high_key.shape
    stack = lambda ref: jnp.concatenate(
        [ref[:, i * groups : (i + 1) * groups].astype(F32) for i in range(8)], axis=0
    )
    picks = stack(nbr_ref)
    upper = jnp.floor(picks * (1.0 / low))
    low_key[...] = picks - upper * low
    place = lax.broadcasted_iota(jnp.int32, (lanes, groups), 0) // slots
    high_key[...] = (upper * 8.0 + place.astype(F32)).T
    edge[...] = stack(weight_ref).T


def prepared(low, nbr, weights):
    slots, atoms = nbr.shape
    lanes, groups = 8 * slots, atoms // 8
    whole = lambda *shape: pl.BlockSpec(shape, lambda: (0,) * len(shape))
    return pl.pallas_call(
        functools.partial(prepare_kernel, low),
        in_specs=[whole(slots, atoms), whole(slots, atoms)],
        out_specs=[pl.BlockSpec(memory_space=pltpu.VMEM)] * 3,
        out_shape=[
            jax.ShapeDtypeStruct((groups, lanes), F32),
            jax.ShapeDtypeStruct((lanes, groups), F32),
            jax.ShapeDtypeStruct((groups, lanes), F32),
        ],
        compiler_params=pltpu.CompilerParams(vmem_limit_bytes=VMEM_LIMIT),
        name="prepared",
    )(*in_hbm(nbr, weights))


def build_adjacency(low, base, span, high_key, low_key, edge, store):
    groups, lanes = high_key.shape
    highs = store.highs
    high_iota = lax.broadcasted_iota(jnp.int32, (highs * 8, lanes), 0).astype(F32).astype(BF16)
    lane = lax.broadcasted_iota(jnp.int32, (lanes, 128), 1).astype(F32)
    low_iota = [(lane + 128.0 * part).astype(BF16) for part in range(low // 128)]
    tile = lambda x, n: jnp.concatenate([x] * (n // 16), axis=0)
    zero = jnp.zeros((), BF16)
    one = jnp.ones((), BF16)
    lane_tile = pl.multiple_of(base // 128 * 128, 128)
    lows = pltpu.roll(low_key[:, pl.ds(lane_tile, 128)], (128 - base % 128) % 128, 1)

    def group(number):
        row = pl.ds(base + number, 1)
        high = jnp.broadcast_to(high_key[row, :], (16, lanes)).astype(BF16)
        value = jnp.broadcast_to(edge[row, :], (16, lanes)).astype(BF16)
        left = jnp.where(tile(high, highs * 8) == high_iota, tile(value, highs * 8), zero)
        lower = jnp.broadcast_to(lows[:, number : number + 1], (lanes, 128)).astype(BF16)
        right = jnp.concatenate([jnp.where(lower == iota, one, zero) for iota in low_iota], axis=1)
        return jnp.dot(left, right, preferred_element_type=F32)

    for number in range(0, span, 2):
        one_group = group(number)
        next_group = group(number + 1)
        for upper in range(highs):
            rows = slice(upper * 8, upper * 8 + 8)
            block = jnp.concatenate([one_group[rows], next_group[rows]], axis=0).astype(BF16)
            store(number * 8, upper, block)


class Store:
    def __init__(self, ref, low):
        self.ref, self.low, self.highs = ref, low, ref.shape[1] // low

    def __call__(self, row, upper, block):
        self.ref[row : row + 16, upper * self.low : (upper + 1) * self.low] = block


def build_kernel(low, span, high_key, low_key, edge, adj_ref):
    build_adjacency(low, pl.program_id(0) * span, span, high_key, low_key, edge, Store(adj_ref, low))


def built(low, keys, rows, here):
    span = min(32, here)
    vmem = pl.BlockSpec(memory_space=pltpu.VMEM)
    return pl.pallas_call(
        functools.partial(build_kernel, low, span),
        grid=(here // span,),
        in_specs=[vmem] * 3,
        out_specs=pl.BlockSpec((8 * span, rows), lambda b: (b, 0)),
        out_shape=pltpu.HBM((8 * here, rows), BF16),
        compiler_params=pltpu.CompilerParams(vmem_limit_bytes=VMEM_LIMIT),
        name="built",
    )(*keys)


def message_kernel(
    low, span, slots, count_ref, adj_hbm, high_key, low_key, edge, own_ref, *refs
):
    halo_refs = [*refs[:4], refs[4].at[0], refs[4].at[1]]
    wmsg_ref, out_ref, slots_ref, msg_ref, sems = refs[-5:]
    atoms, width = own_ref.shape
    groups = high_key.shape[0]
    step = pl.program_id(0)
    steps = pl.num_programs(0)
    early = sems.shape[0]

    def fetch(piece):
        rows = pl.ds(piece * 8 * span, 8 * span)
        return pltpu.make_async_copy(adj_hbm.at[rows], slots_ref.at[piece + 1], sems.at[piece])

    @pl.when(step == 0)
    def _():
        for piece in range(early):
            fetch(piece).start()

    for piece in range(early):

        @pl.when(step == steps - early + piece)
        def _():
            fetch(piece).wait()

    @pl.when(step < steps - early)
    def _():
        start = (step + early) * span
        build_adjacency(low, start, span, high_key, low_key, edge, Store(slots_ref.at[0], low))

    base = lax.rem(step + early, steps) * span
    adj_ref = slots_ref.at[jnp.maximum(step + early - steps + 1, 0)]
    summed = jnp.dot(adj_ref[:, :atoms], own_ref[...], preferred_element_type=F32)
    halo = jnp.concatenate([ref[...] for ref in halo_refs], axis=0)
    summed += jnp.dot(adj_ref[:, atoms:], halo, preferred_element_type=F32)
    message = (summed / math.sqrt(slots)).astype(BF16)
    hidden = jnp.dot(message, wmsg_ref[...], preferred_element_type=F32)
    msg_ref[...] = hidden / (1.0 + jnp.exp(-hidden))
    inside = pl.multiple_of(base, span)
    for i in range(8):
        start = pl.multiple_of(i * groups + inside, span)
        own = own_ref[pl.ds(start, span), :].astype(F32)
        gate = msg_ref[pl.ds(i, span, stride=8), :]
        atom = lax.broadcasted_iota(jnp.int32, (span, width), 0) + start
        out_ref[i] = jnp.where(atom < count_ref[0], own + gate, 0.0).astype(BF16)


def messages(low, count, adjacency, keys, own, halos, wmsg, slots):
    groups = keys[0].shape[0]
    atoms, width = own.shape
    rows = adjacency.shape[1]
    span = min(64, groups // 2)
    vmem = pl.BlockSpec(memory_space=pltpu.VMEM)
    arrays = [*keys, own, *halos, wmsg]
    steps = groups // span
    early = adjacency.shape[0] // (8 * span)
    out = pl.pallas_call(
        functools.partial(message_kernel, low, span, slots),
        grid=(steps,),
        in_specs=[pl.BlockSpec(memory_space=pltpu.SMEM), pl.BlockSpec(memory_space=pltpu.HBM)]
        + [vmem] * len(arrays),
        out_specs=pl.BlockSpec((8, span, width), lambda b: (0, lax.rem(b + early, steps), 0)),
        out_shape=jax.ShapeDtypeStruct((8, groups, width), BF16),
        scratch_shapes=[
            pltpu.VMEM((1 + early, 8 * span, rows), BF16),
            pltpu.VMEM((8 * span, width), F32),
            pltpu.SemaphoreType.DMA((early,)),
        ],
        cost_estimate=pl.CostEstimate(flops=10**10, transcendentals=0, bytes_accessed=10**7),
        compiler_params=pltpu.CompilerParams(vmem_limit_bytes=20 << 20),
        name="messages",
    )(count, *in_hbm(adjacency), *arrays)
    return out.reshape(atoms, width)


def back_kernel(scale, count_ref, table_hbm, *refs):
    *g_refs, out_ref, table_ref, sems = refs
    atoms, width = out_ref.shape
    pieces = sems.shape[0]
    rows = atoms // pieces
    copies = []
    for piece in range(pieces):
        here = pl.ds(piece * rows, rows)
        copies.append(pltpu.make_async_copy(table_hbm.at[here], table_ref.at[here], sems.at[piece]))
        copies[-1].start()
    for piece in range(pieces):
        copies[piece].wait()
        here = slice(piece * rows, (piece + 1) * rows)
        back = jnp.zeros((rows, width), F32)
        start = 0
        for g_ref in g_refs:
            depth = g_ref.shape[0]
            back += jnp.dot(
                table_ref[here, start : start + depth], g_ref[...], preferred_element_type=F32
            )
            start += depth
        atom = lax.broadcasted_iota(jnp.int32, (rows, width), 0) + piece * rows
        out_ref[here, :] = jnp.where(atom < count_ref[0], back * scale, 0.0)


def back(count, table, gs, scale):
    atoms, depth = table.shape
    width = gs[0].shape[1]
    vmem = pl.BlockSpec(memory_space=pltpu.VMEM)
    return pl.pallas_call(
        functools.partial(back_kernel, scale),
        in_specs=[
            pl.BlockSpec(memory_space=pltpu.SMEM),
            pl.BlockSpec(memory_space=pltpu.HBM),
            *[vmem for _ in gs],
        ],
        out_specs=vmem,
        out_shape=jax.ShapeDtypeStruct((atoms, width), F32),
        scratch_shapes=[pltpu.VMEM((atoms, depth), BF16), pltpu.SemaphoreType.DMA((8,))],
        compiler_params=pltpu.CompilerParams(vmem_limit_bytes=VMEM_LIMIT),
        name="back",
    )(count, *in_hbm(table), *gs)


def passed_along(value, axis, steps):
    size = lax.axis_size(axis)
    pairs = [(source, (source + steps) % size) for source in range(size)]
    return lax.ppermute(value, axis, pairs)


def shards(
    features, positions, counts, kvec, sigma, w_mix, neighbours, edge_weight, send_list, w_message
):
    atoms = features.shape[3]
    width = features.shape[4]
    kcount = kvec.shape[1]
    slots = neighbours.shape[3]
    feats = features.reshape(atoms, width)
    count = counts.reshape(1)
    sizes = [lax.axis_size(axis) for axis in ("gx", "gy", "gz")]
    plane = sizes[0] * sizes[1]
    devices = plane * sizes[2]
    place = jnp.stack([lax.axis_index(axis) for axis in ("gx", "gy", "gz")]).astype(jnp.int32)
    paired = sizes[2] == 2

    scale = 1.0 / math.sqrt(atoms * devices)
    table, *sums = phases(
        place, count, sizes, scale, positions.reshape(3, atoms), feats, kvec, sigma, w_mix
    )
    low = 256
    nbr, _ = lax.optimization_barrier((neighbours.reshape(slots, atoms), sums))
    keys = prepared(low, nbr, edge_weight.reshape(slots, atoms))
    if paired:
        mine = sums[1] + passed_along(sums[0], "gz", 1)
    else:
        parts = lax.all_to_all(sums[0], "gz", 0, 0, tiled=True)
        mine = jnp.sum(parts.reshape(sizes[2], -1, width), axis=0)
    part = mine.shape[0] // plane
    mine, keys, send, feats = lax.optimization_barrier((mine, keys, send_list, feats))

    received = lax.all_to_all(mine.reshape(plane, part, width), ("gx", "gy"), 0, 0, tiled=True)
    *outgoing, own = selected(count, send.reshape(6, 1, -1), feats)
    halos = [
        passed_along(outgoing[2 * number + side], axis, 1 - 2 * side)
        for number, axis in enumerate(("gx", "gy"))
        for side in range(2)
    ]
    if paired:
        halos.append(passed_along(outgoing[4], "gz", 1))
    else:
        halos.append(jnp.stack([passed_along(outgoing[4][side], "gz", 1 - 2 * side) for side in range(2)]))
    adjacency = built(low, keys, atoms + send.size, atoms // 8 // 4 * EARLY)
    received, halos, adjacency = lax.optimization_barrier((received, halos, adjacency))

    shares = totals(received)
    g = lax.all_to_all(shares, ("gx", "gy"), 0, 0, tiled=True).reshape(plane * part, width)
    halos, _ = lax.optimization_barrier((halos, shares))
    updated = messages(low, count, adjacency, keys, own, halos, w_message, slots)
    g, updated = lax.optimization_barrier((g, updated))
    if paired:
        gs = [passed_along(g, "gz", 1), g]
    else:
        gs = [lax.all_gather(g, "gz", tiled=True)]
    long_range = back(count, table, gs, 2.0 / math.sqrt(kcount))
    return (updated.reshape(1, 1, 1, atoms, width), long_range.reshape(1, 1, 1, atoms, width))


def solution(mesh):
    split = P("gx", "gy", "gz", None, None)
    placed = (split, split, P("gx", "gy", "gz"), P(), P(), P(), split, split, split, P())
    return jax.shard_map(
        shards, mesh=mesh, in_specs=placed, out_specs=(split, split), check_vma=False
    )
```

```python
import functools
import math

import jax
import jax.numpy as jnp
import numpy as np
from jax import lax
from jax.experimental import pallas as pl
from jax.experimental.pallas import tpu as pltpu
from jax.sharding import PartitionSpec as P

F32 = jnp.float32
BF16 = jnp.bfloat16
VMEM_LIMIT = 14 << 20
EARLY = 2


def half_turn_series():
    angle = np.cos((np.arange(400) + 0.5) * np.pi / 800)
    r = 0.5 * angle
    u = r * r
    root = math.sqrt(2.0)
    even = np.polynomial.chebyshev.Chebyshev.fit(u, root * np.cos(np.pi * r), 4, domain=[0, 0.25])
    odd = np.polynomial.chebyshev.Chebyshev.fit(u, root * np.sin(np.pi * r) / r, 4, domain=[0, 0.25])
    take = lambda fit: [float(v) for v in fit.convert(kind=np.polynomial.Polynomial).coef]
    return take(even), take(odd)


EVEN, ODD = half_turn_series()


def in_hbm(*values):
    return [pltpu.with_memory_space_constraint(value, pltpu.HBM) for value in values]


def horner(coefs, u):
    total = coefs[-1] * u + coefs[-2]
    for coef in coefs[-3::-1]:
        total = total * u + coef
    return total


def phase_kernel(
    sizes,
    scale,
    paired,
    place_ref,
    count_ref,
    pos_ref,
    feat_ref,
    kvec_ref,
    sigma_ref,
    mix_ref,
    table_ref,
    *refs,
):
    out_refs = refs[: 1 + paired]
    frac_ref, own_ref, mix_turned, decay_ref, block_ref, sems = refs[1 + paired :]
    atoms, width = feat_ref.shape
    kblock = kvec_ref.shape[1]
    step = pl.program_id(0)

    @pl.when(step == 0)
    def _():
        rows = []
        for axis in range(3):
            frac = (place_ref[axis].astype(F32) + pos_ref[axis]) / sizes[axis]
            high = frac.astype(BF16).astype(F32)
            middle = (frac - high).astype(BF16).astype(F32)
            rows += [high, middle, frac - high - middle]
        stacked = jnp.concatenate(rows + [jnp.zeros((16 - len(rows), atoms), F32)], axis=0)
        frac_ref[...] = stacked.T.astype(BF16)
        atom = lax.broadcasted_iota(jnp.int32, (atoms, width), 0)
        own = jnp.where(atom < count_ref[0], feat_ref[...].astype(F32), 0.0)
        own_ref[...] = own.T.astype(BF16)
        mix_turned[...] = mix_ref[...].T
        decay_ref[...] = jnp.broadcast_to(-sigma_ref[...], (width, width)).T

    kvec = kvec_ref[...].astype(F32)
    weights = jnp.concatenate(
        [kvec[axis : axis + 1, :] for axis in range(3) for _ in range(3)]
        + [jnp.zeros((7, kblock), F32)],
        axis=0,
    ).astype(BF16)
    chunk = atoms // sems.shape[1]
    slot = lax.rem(step, 2)

    def store(number, which, column):
        rows = pl.ds(number * chunk, chunk)
        columns = pl.ds(pl.multiple_of(column * 2 * kblock, 2 * kblock), 2 * kblock)
        return pltpu.make_async_copy(
            block_ref.at[which, rows], table_ref.at[rows, columns], sems.at[which, number]
        )

    @pl.when(step >= 2)
    def _():
        for number in range(atoms // chunk):
            store(number, slot, step - 2).wait()

    for start in range(0, atoms, chunk):
        rows = slice(start, start + chunk)
        theta = jnp.dot(frac_ref[rows, :], weights, preferred_element_type=F32)
        r = theta - jnp.round(theta)
        u = r * r
        even = horner(EVEN, u)
        odd = horner(ODD, u) * r
        cosine = (1.0 - odd * odd).astype(BF16)
        sine = (even * odd).astype(BF16)
        block_ref[slot, rows, :kblock] = cosine
        block_ref[slot, rows, kblock:] = sine
        store(start // chunk, slot, step).start()

    sums = jnp.dot(own_ref[...], block_ref[slot], preferred_element_type=F32)
    ksq = jnp.sum(kvec * kvec, axis=0, keepdims=True)
    decay = jnp.exp(decay_ref[:, :1] * ksq)
    mixed = jnp.dot(
        mix_turned[...], sums * scale, precision=lax.Precision.HIGHEST, preferred_element_type=F32
    )
    result = (mixed * jnp.concatenate([decay, decay], axis=1)).T
    if paired:
        half = pl.num_programs(0) // 2

        @pl.when(step < half)
        def _():
            out_refs[0][...] = result

        @pl.when(step >= half)
        def _():
            out_refs[1][...] = result
    else:
        out_refs[0][...] = result

    @pl.when(step == pl.num_programs(0) - 1)
    def _():
        for number in range(atoms // chunk):
            store(number, 1 - slot, step - 1).wait()
            store(number, slot, step).wait()


def phases(place, count, sizes, scale, pos, feats, kvec, sigma, w_mix):
    atoms, width = feats.shape
    kcount = kvec.shape[1]
    kblock = 256 if kcount % 512 == 0 else 128
    steps = kcount // kblock
    half = steps // 2
    paired = sizes[2] == 2
    whole = lambda *shape: pl.BlockSpec(shape, lambda b, *_: (0,) * len(shape))

    def kvec_map(b, place_ref, count_ref):
        return (0, lax.rem(b + (1 - place_ref[2]) * half, steps) if paired else b)

    if paired:
        out_specs = [
            pl.BlockSpec((2 * kblock, width), lambda b, *_: (jnp.minimum(b, half - 1), 0)),
            pl.BlockSpec((2 * kblock, width), lambda b, *_: (jnp.maximum(b - half, 0), 0)),
        ]
        out_shape = [jax.ShapeDtypeStruct((kcount, width), F32)] * 2
    else:
        out_specs = [pl.BlockSpec((2 * kblock, width), lambda b, *_: (b, 0))]
        out_shape = [jax.ShapeDtypeStruct((2 * kcount, width), F32)]
    return pl.pallas_call(
        functools.partial(phase_kernel, sizes, scale, paired),
        grid_spec=pltpu.PrefetchScalarGridSpec(
            num_scalar_prefetch=2,
            grid=(steps,),
            in_specs=[
                whole(3, 1, atoms),
                whole(atoms, width),
                pl.BlockSpec((3, kblock), kvec_map),
                whole(1, width),
                whole(width, width),
            ],
            out_specs=[pl.BlockSpec(memory_space=pltpu.HBM), *out_specs],
            scratch_shapes=[
                pltpu.VMEM((atoms, 16), BF16),
                pltpu.VMEM((width, atoms), BF16),
                pltpu.VMEM((width, width), F32),
                pltpu.VMEM((width, width), F32),
                pltpu.VMEM((2, atoms, 2 * kblock), BF16),
                pltpu.SemaphoreType.DMA((2, 8)),
            ],
        ),
        out_shape=[pltpu.HBM((atoms, 2 * kcount), BF16), *out_shape],
        compiler_params=pltpu.CompilerParams(vmem_limit_bytes=VMEM_LIMIT),
        name="phases",
    )(place, count, *in_hbm(pos.reshape(3, 1, atoms), feats, kvec, sigma.reshape(1, width), w_mix))


def select_kernel(count_ref, send_ref, feat_ref, *refs):
    *out_refs, own_ref = refs
    faces, _, picks = send_ref.shape
    atoms, width = feat_ref.shape
    atom = lax.broadcasted_iota(jnp.int32, (atoms, width), 0)
    own_ref[...] = jnp.where(atom < count_ref[0], feat_ref[...].astype(F32), 0.0).astype(BF16)
    rows = jnp.concatenate([send_ref[face] for face in range(faces)], axis=0).astype(F32)
    columns = jnp.concatenate([rows, jnp.zeros((8 - faces, picks), F32)], axis=0).T
    chunk = min(256, atoms)
    lane = lax.broadcasted_iota(jnp.int32, (picks, chunk), 1).astype(F32).astype(BF16)
    one, zero = jnp.ones((), BF16), jnp.zeros((), BF16)
    for face in range(faces):
        spread = jnp.broadcast_to(columns[:, face : face + 1], (picks, 128))
        total = jnp.zeros((picks, width), F32)
        for start in range(0, atoms, chunk):
            key = (spread - float(start)).astype(BF16)
            hot = jnp.where(jnp.concatenate([key] * (chunk // 128), axis=1) == lane, one, zero)
            total += jnp.dot(hot, own_ref[start : start + chunk, :], preferred_element_type=F32)
        if face < 4:
            out_refs[face][...] = total.astype(BF16)
        else:
            out_refs[4][face - 4] = total.astype(BF16)


def selected(count, send, feats):
    atoms, width = feats.shape
    faces, _, picks = send.shape
    return pl.pallas_call(
        select_kernel,
        in_specs=[
            pl.BlockSpec(memory_space=pltpu.SMEM),
            pl.BlockSpec((faces, 1, picks), lambda: (0, 0, 0)),
            pl.BlockSpec((atoms, width), lambda: (0, 0)),
        ],
        out_specs=[pl.BlockSpec(memory_space=pltpu.VMEM)] * 6,
        out_shape=[jax.ShapeDtypeStruct((picks, width), BF16)] * 4
        + [jax.ShapeDtypeStruct((2, picks, width), BF16), jax.ShapeDtypeStruct((atoms, width), BF16)],
        compiler_params=pltpu.CompilerParams(vmem_limit_bytes=VMEM_LIMIT),
        name="selected",
    )(count, *in_hbm(send, feats))


def total_kernel(parts_ref, out_ref):
    total = parts_ref[0].astype(F32)
    for part in range(1, parts_ref.shape[0]):
        total += parts_ref[part].astype(F32)
    total = total.astype(BF16)
    for part in range(parts_ref.shape[0]):
        out_ref[part] = total


def totals(parts):
    return pl.pallas_call(
        total_kernel,
        in_specs=[pl.BlockSpec(memory_space=pltpu.VMEM)],
        out_specs=pl.BlockSpec(memory_space=pltpu.VMEM),
        out_shape=jax.ShapeDtypeStruct(parts.shape, BF16),
        compiler_params=pltpu.CompilerParams(vmem_limit_bytes=4 << 20),
        name="totals",
    )(parts)


def prepare_kernel(low, nbr_ref, weight_ref, wmsg_ref, high_key, low_key, edge, wmsg_out):
    wmsg_out[...] = wmsg_ref[...]
    slots, atoms = nbr_ref.shape
    groups, lanes = high_key.shape
    stack = lambda ref: jnp.concatenate(
        [ref[:, i * groups : (i + 1) * groups].astype(F32) for i in range(8)], axis=0
    )
    picks = stack(nbr_ref)
    upper = jnp.floor(picks * (1.0 / low))
    low_key[...] = picks - upper * low
    place = lax.broadcasted_iota(jnp.int32, (lanes, groups), 0) // slots
    high_key[...] = (upper * 8.0 + place.astype(F32)).T
    edge[...] = stack(weight_ref).T


def prepared(low, nbr, weights, wmsg):
    slots, atoms = nbr.shape
    lanes, groups = 8 * slots, atoms // 8
    whole = lambda *shape: pl.BlockSpec(shape, lambda: (0,) * len(shape))
    return pl.pallas_call(
        functools.partial(prepare_kernel, low),
        in_specs=[whole(slots, atoms), whole(slots, atoms), whole(*wmsg.shape)],
        out_specs=[pl.BlockSpec(memory_space=pltpu.VMEM)] * 4,
        out_shape=[
            jax.ShapeDtypeStruct((groups, lanes), F32),
            jax.ShapeDtypeStruct((lanes, groups), F32),
            jax.ShapeDtypeStruct((groups, lanes), F32),
            jax.ShapeDtypeStruct(wmsg.shape, BF16),
        ],
        compiler_params=pltpu.CompilerParams(vmem_limit_bytes=VMEM_LIMIT),
        name="prepared",
    )(*in_hbm(nbr, weights, wmsg))


def build_adjacency(low, base, span, high_key, low_key, edge, store):
    groups, lanes = high_key.shape
    highs = store.highs
    high_iota = lax.broadcasted_iota(jnp.int32, (highs * 8, lanes), 0).astype(F32).astype(BF16)
    lane = lax.broadcasted_iota(jnp.int32, (lanes, 128), 1).astype(F32)
    low_iota = [(lane + 128.0 * part).astype(BF16) for part in range(low // 128)]
    tile = lambda x, n: jnp.concatenate([x] * (n // 16), axis=0)
    zero = jnp.zeros((), BF16)
    one = jnp.ones((), BF16)
    lane_tile = pl.multiple_of(base // 128 * 128, 128)
    lows = pltpu.roll(low_key[:, pl.ds(lane_tile, 128)], (128 - base % 128) % 128, 1)

    def group(number):
        row = pl.ds(base + number, 1)
        high = jnp.broadcast_to(high_key[row, :], (16, lanes)).astype(BF16)
        value = jnp.broadcast_to(edge[row, :], (16, lanes)).astype(BF16)
        left = jnp.where(tile(high, highs * 8) == high_iota, tile(value, highs * 8), zero)
        lower = jnp.broadcast_to(lows[:, number : number + 1], (lanes, 128)).astype(BF16)
        right = jnp.concatenate([jnp.where(lower == iota, one, zero) for iota in low_iota], axis=1)
        return jnp.dot(left, right, preferred_element_type=F32)

    for number in range(0, span, 2):
        one_group = group(number)
        next_group = group(number + 1)
        for upper in range(highs):
            rows = slice(upper * 8, upper * 8 + 8)
            block = jnp.concatenate([one_group[rows], next_group[rows]], axis=0).astype(BF16)
            store(number * 8, upper, block)


class Store:
    def __init__(self, own_ref, halo_ref, low):
        self.own_ref, self.halo_ref, self.low = own_ref, halo_ref, low
        self.split = own_ref.shape[1] // low
        self.highs = self.split + halo_ref.shape[1] // low

    def __call__(self, row, upper, block):
        ref = self.own_ref if upper < self.split else self.halo_ref
        upper -= 0 if upper < self.split else self.split
        ref[row : row + 16, upper * self.low : (upper + 1) * self.low] = block


def build_kernel(low, span, high_key, low_key, edge, own_ref, halo_adj, partial_ref, own_adj):
    store = Store(own_adj, halo_adj, low)
    build_adjacency(low, pl.program_id(0) * span, span, high_key, low_key, edge, store)
    partial_ref[...] = jnp.dot(own_adj[...], own_ref[...], preferred_element_type=F32)


def built(low, keys, own, halo_rows, here):
    atoms, width = own.shape
    span = min(64, here)
    vmem = pl.BlockSpec(memory_space=pltpu.VMEM)
    return pl.pallas_call(
        functools.partial(build_kernel, low, span),
        grid=(here // span,),
        in_specs=[vmem] * 4,
        out_specs=[
            pl.BlockSpec((8 * span, halo_rows), lambda b: (b, 0)),
            pl.BlockSpec((8 * span, width), lambda b: (b, 0)),
        ],
        out_shape=[pltpu.HBM((8 * here, halo_rows), BF16), jax.ShapeDtypeStruct((8 * here, width), F32)],
        scratch_shapes=[pltpu.VMEM((8 * span, atoms), BF16)],
        compiler_params=pltpu.CompilerParams(vmem_limit_bytes=VMEM_LIMIT),
        name="built",
    )(*keys, own)


def message_kernel(
    low, span, slots, early, count_ref, early_hbm, partial_ref, high_key, low_key, edge, own_ref, *refs
):
    halo_refs = [*refs[:4], refs[4].at[0], refs[4].at[1]]
    wmsg_ref, out_ref, early_adj, own_adj, halo_adj, msg_ref, sem = refs[-7:]
    atoms, width = own_ref.shape
    groups = high_key.shape[0]
    step = pl.program_id(0)
    steps = pl.num_programs(0)
    halo = jnp.concatenate([ref[...] for ref in halo_refs], axis=0)
    fetch = pltpu.make_async_copy(early_hbm, early_adj, sem)

    @pl.when(step == 0)
    def _():
        fetch.start()

    @pl.when(step == steps - early)
    def _():
        fetch.wait()

    @pl.when(step < steps - early)
    def _():
        store = Store(own_adj, halo_adj, low)
        build_adjacency(low, (step + early) * span, span, high_key, low_key, edge, store)
        summed = jnp.dot(own_adj[...], own_ref[...], preferred_element_type=F32)
        msg_ref[...] = summed + jnp.dot(halo_adj[...], halo, preferred_element_type=F32)

    @pl.when(step >= steps - early)
    def _():
        rows = pl.ds(pl.multiple_of((step + early - steps) * 8 * span, 8 * span), 8 * span)
        more = jnp.dot(early_adj[rows, :], halo, preferred_element_type=F32)
        msg_ref[...] = partial_ref[rows, :] + more

    message = (msg_ref[...] / math.sqrt(slots)).astype(BF16)
    hidden = jnp.dot(message, wmsg_ref[...], preferred_element_type=F32)
    msg_ref[...] = hidden / (1.0 + jnp.exp(-hidden))
    inside = pl.multiple_of(lax.rem(step + early, steps) * span, span)
    for i in range(8):
        start = pl.multiple_of(i * groups + inside, span)
        own = own_ref[pl.ds(start, span), :].astype(F32)
        gate = msg_ref[pl.ds(i, span, stride=8), :]
        atom = lax.broadcasted_iota(jnp.int32, (span, width), 0) + start
        out_ref[i] = jnp.where(atom < count_ref[0], own + gate, 0.0).astype(BF16)


def messages(low, count, early_adj, partial, keys, own, halos, wmsg, slots):
    groups = keys[0].shape[0]
    atoms, width = own.shape
    halo_rows = early_adj.shape[1]
    span = min(64, groups // 4)
    vmem = pl.BlockSpec(memory_space=pltpu.VMEM)
    arrays = [partial, *keys, own, *halos, wmsg]
    steps = groups // span
    early = early_adj.shape[0] // (8 * span)
    out = pl.pallas_call(
        functools.partial(message_kernel, low, span, slots, early),
        grid=(steps,),
        in_specs=[pl.BlockSpec(memory_space=pltpu.SMEM), pl.BlockSpec(memory_space=pltpu.HBM)]
        + [vmem] * len(arrays),
        out_specs=pl.BlockSpec((8, span, width), lambda b: (0, lax.rem(b + early, steps), 0)),
        out_shape=jax.ShapeDtypeStruct((8, groups, width), BF16),
        scratch_shapes=[
            pltpu.VMEM(early_adj.shape, BF16),
            pltpu.VMEM((8 * span, atoms), BF16),
            pltpu.VMEM((8 * span, halo_rows), BF16),
            pltpu.VMEM((8 * span, width), F32),
            pltpu.SemaphoreType.DMA,
        ],
        compiler_params=pltpu.CompilerParams(vmem_limit_bytes=VMEM_LIMIT),
        name="messages",
    )(count, *in_hbm(early_adj), *arrays)
    return out.reshape(atoms, width)


def back_kernel(scale, count_ref, table_hbm, *refs):
    *g_refs, out_hbm, table_ref, out_ref, sems, out_sems = refs
    atoms, width = out_ref.shape
    pieces = sems.shape[0]
    rows = atoms // pieces
    copies = []
    for piece in range(pieces):
        here = pl.ds(piece * rows, rows)
        copies.append(pltpu.make_async_copy(table_hbm.at[here], table_ref.at[here], sems.at[piece]))
        copies[-1].start()
    for piece in range(pieces):
        copies[piece].wait()
        here = slice(piece * rows, (piece + 1) * rows)
        back = jnp.zeros((rows, width), F32)
        start = 0
        for g_ref in g_refs:
            depth = g_ref.shape[0]
            back += jnp.dot(
                table_ref[here, start : start + depth], g_ref[...], preferred_element_type=F32
            )
            start += depth
        atom = lax.broadcasted_iota(jnp.int32, (rows, width), 0) + piece * rows
        out_ref[here, :] = jnp.where(atom < count_ref[0], back * scale, 0.0)
        here = pl.ds(piece * rows, rows)
        copies.append(pltpu.make_async_copy(out_ref.at[here], out_hbm.at[here], out_sems.at[piece]))
        copies[-1].start()
    for copy in copies[pieces:]:
        copy.wait()


def back(count, table, gs, scale):
    atoms, depth = table.shape
    width = gs[0].shape[1]
    vmem = pl.BlockSpec(memory_space=pltpu.VMEM)
    return pl.pallas_call(
        functools.partial(back_kernel, scale),
        in_specs=[
            pl.BlockSpec(memory_space=pltpu.SMEM),
            pl.BlockSpec(memory_space=pltpu.HBM),
            *[vmem for _ in gs],
        ],
        out_specs=pl.BlockSpec(memory_space=pltpu.HBM),
        out_shape=pltpu.HBM((atoms, width), F32),
        scratch_shapes=[
            pltpu.VMEM((atoms, depth), BF16),
            pltpu.VMEM((atoms, width), F32),
            pltpu.SemaphoreType.DMA((8,)),
            pltpu.SemaphoreType.DMA((8,)),
        ],
        compiler_params=pltpu.CompilerParams(vmem_limit_bytes=VMEM_LIMIT),
        name="back",
    )(count, *in_hbm(table), *gs)


def passed_along(value, axis, steps):
    size = lax.axis_size(axis)
    pairs = [(source, (source + steps) % size) for source in range(size)]
    return lax.ppermute(value, axis, pairs)


def shards(
    features, positions, counts, kvec, sigma, w_mix, neighbours, edge_weight, send_list, w_message
):
    atoms = features.shape[3]
    width = features.shape[4]
    kcount = kvec.shape[1]
    slots = neighbours.shape[3]
    feats = features.reshape(atoms, width)
    count = counts.reshape(1)
    sizes = [lax.axis_size(axis) for axis in ("gx", "gy", "gz")]
    plane = sizes[0] * sizes[1]
    devices = plane * sizes[2]
    place = jnp.stack([lax.axis_index(axis) for axis in ("gx", "gy", "gz")]).astype(jnp.int32)
    paired = sizes[2] == 2

    scale = 1.0 / math.sqrt(atoms * devices)
    table, *sums = phases(
        place, count, sizes, scale, positions.reshape(3, atoms), feats, kvec, sigma, w_mix
    )
    low = 256
    nbr, _ = lax.optimization_barrier((neighbours.reshape(slots, atoms), sums))
    *keys, wmsg = prepared(low, nbr, edge_weight.reshape(slots, atoms), w_message)
    if paired:
        mine = sums[1] + passed_along(sums[0], "gz", 1)
    else:
        parts = lax.all_to_all(sums[0], "gz", 0, 0, tiled=True)
        mine = jnp.sum(parts.reshape(sizes[2], -1, width), axis=0)
    part = mine.shape[0] // plane
    mine, keys, wmsg, send, feats = lax.optimization_barrier((mine, keys, wmsg, send_list, feats))

    received = lax.all_to_all(mine.reshape(plane, part, width), ("gx", "gy"), 0, 0, tiled=True)
    *outgoing, own = selected(count, send.reshape(6, 1, -1), feats)
    halos = [
        passed_along(outgoing[2 * number + side], axis, 1 - 2 * side)
        for number, axis in enumerate(("gx", "gy"))
        for side in range(2)
    ]
    if paired:
        halos.append(passed_along(outgoing[4], "gz", 1))
    else:
        halos.append(jnp.stack([passed_along(outgoing[4][side], "gz", 1 - 2 * side) for side in range(2)]))
    adjacency = built(low, keys, own, send.size, atoms // 8 // 4 * EARLY)
    received, halos, adjacency = lax.optimization_barrier((received, halos, adjacency))

    shares = totals(received)
    g = lax.all_to_all(shares, ("gx", "gy"), 0, 0, tiled=True).reshape(plane * part, width)
    halos, _ = lax.optimization_barrier((halos, shares))
    updated = messages(low, count, *adjacency, keys, own, halos, wmsg, slots)
    g, updated = lax.optimization_barrier((g, updated))
    if paired:
        gs = [passed_along(g, "gz", 1), g]
    else:
        gs = [lax.all_gather(g, "gz", tiled=True)]
    long_range = back(count, table, gs, 2.0 / math.sqrt(kcount))
    return (updated.reshape(1, 1, 1, atoms, width), long_range.reshape(1, 1, 1, atoms, width))


def solution(mesh):
    split = P("gx", "gy", "gz", None, None)
    placed = (split, split, P("gx", "gy", "gz"), P(), P(), P(), split, split, split, P())
    return jax.shard_map(
        shards, mesh=mesh, in_specs=placed, out_specs=(split, split), check_vma=False
    )
```

```python
import functools
import math

import jax
import jax.numpy as jnp
import numpy as np
from jax import lax
from jax.experimental import pallas as pl
from jax.experimental.pallas import tpu as pltpu
from jax.sharding import PartitionSpec as P

F32 = jnp.float32
BF16 = jnp.bfloat16
VMEM_LIMIT = 18 << 20
EARLY = 2


def half_turn_series():
    angle = np.cos((np.arange(400) + 0.5) * np.pi / 800)
    r = 0.5 * angle
    u = r * r
    root = math.sqrt(2.0)
    even = np.polynomial.chebyshev.Chebyshev.fit(u, root * np.cos(np.pi * r), 4, domain=[0, 0.25])
    odd = np.polynomial.chebyshev.Chebyshev.fit(u, root * np.sin(np.pi * r) / r, 4, domain=[0, 0.25])
    take = lambda fit: [float(v) for v in fit.convert(kind=np.polynomial.Polynomial).coef]
    return take(even), take(odd)


EVEN, ODD = half_turn_series()


def in_hbm(*values):
    return [pltpu.with_memory_space_constraint(value, pltpu.HBM) for value in values]


def horner(coefs, u):
    total = coefs[-1] * u + coefs[-2]
    for coef in coefs[-3::-1]:
        total = total * u + coef
    return total


def phase_kernel(
    sizes,
    scale,
    paired,
    place_ref,
    count_ref,
    pos_ref,
    feat_ref,
    kvec_ref,
    sigma_ref,
    mix_ref,
    table_ref,
    live_ref,
    *refs,
):
    out_refs = refs[: 1 + paired]
    frac_ref, own_ref, mix_turned, decay_ref, block_ref, sems = refs[1 + paired :]
    atoms, width = feat_ref.shape
    kblock = kvec_ref.shape[1]
    step = pl.program_id(0)

    @pl.when(step == 0)
    def _():
        rows = []
        for axis in range(3):
            frac = (place_ref[axis].astype(F32) + pos_ref[axis]) / sizes[axis]
            high = frac.astype(BF16).astype(F32)
            middle = (frac - high).astype(BF16).astype(F32)
            rows += [high, middle, frac - high - middle]
        stacked = jnp.concatenate(rows + [jnp.zeros((16 - len(rows), atoms), F32)], axis=0)
        frac_ref[...] = stacked.T.astype(BF16)
        atom = lax.broadcasted_iota(jnp.int32, (atoms, width), 0)
        own = jnp.where(atom < count_ref[0], feat_ref[...].astype(F32), 0.0)
        own_ref[...] = own.T.astype(BF16)
        live_ref[...] = own.astype(BF16)
        mix_turned[...] = mix_ref[...].T
        decay_ref[...] = jnp.broadcast_to(-sigma_ref[...], (width, width)).T

    kvec = kvec_ref[...].astype(F32)
    weights = jnp.concatenate(
        [kvec[axis : axis + 1, :] for axis in range(3) for _ in range(3)]
        + [jnp.zeros((7, kblock), F32)],
        axis=0,
    ).astype(BF16)
    chunk = atoms // sems.shape[1]
    slot = lax.rem(step, 2)

    def store(number, which, column):
        rows = pl.ds(number * chunk, chunk)
        columns = pl.ds(pl.multiple_of(column * 2 * kblock, 2 * kblock), 2 * kblock)
        return pltpu.make_async_copy(
            block_ref.at[which, rows], table_ref.at[rows, columns], sems.at[which, number]
        )

    @pl.when(step >= 2)
    def _():
        for number in range(atoms // chunk):
            store(number, slot, step - 2).wait()

    for start in range(0, atoms, chunk):
        rows = slice(start, start + chunk)
        theta = jnp.dot(frac_ref[rows, :], weights, preferred_element_type=F32)
        r = theta - jnp.round(theta)
        u = r * r
        even = horner(EVEN, u)
        odd = horner(ODD, u) * r
        cosine = (1.0 - odd * odd).astype(BF16)
        sine = (even * odd).astype(BF16)
        block_ref[slot, rows, :kblock] = cosine
        block_ref[slot, rows, kblock:] = sine
        store(start // chunk, slot, step).start()

    sums = jnp.dot(own_ref[...], block_ref[slot], preferred_element_type=F32)
    ksq = jnp.sum(kvec * kvec, axis=0, keepdims=True)
    decay = jnp.exp(decay_ref[:, :1] * ksq)
    mixed = jnp.dot(
        mix_turned[...], sums * scale, precision=lax.Precision.HIGHEST, preferred_element_type=F32
    )
    result = (mixed * jnp.concatenate([decay, decay], axis=1)).T
    if paired:
        half = pl.num_programs(0) // 2

        @pl.when(step < half)
        def _():
            out_refs[0][...] = result

        @pl.when(step >= half)
        def _():
            out_refs[1][...] = result
    else:
        out_refs[0][...] = result

    @pl.when(step == pl.num_programs(0) - 1)
    def _():
        for number in range(atoms // chunk):
            store(number, 1 - slot, step - 1).wait()
            store(number, slot, step).wait()


def phases(place, count, sizes, scale, pos, feats, kvec, sigma, w_mix):
    atoms, width = feats.shape
    kcount = kvec.shape[1]
    kblock = 512 if kcount % 1024 == 0 else 128
    steps = kcount // kblock
    half = steps // 2
    paired = sizes[2] == 2
    whole = lambda *shape: pl.BlockSpec(shape, lambda b, *_: (0,) * len(shape))

    def kvec_map(b, place_ref, count_ref):
        return (0, lax.rem(b + (1 - place_ref[2]) * half, steps) if paired else b)

    if paired:
        out_specs = [
            pl.BlockSpec((2 * kblock, width), lambda b, *_: (jnp.minimum(b, half - 1), 0)),
            pl.BlockSpec((2 * kblock, width), lambda b, *_: (jnp.maximum(b - half, 0), 0)),
        ]
        out_shape = [jax.ShapeDtypeStruct((kcount, width), F32)] * 2
    else:
        out_specs = [pl.BlockSpec((2 * kblock, width), lambda b, *_: (b, 0))]
        out_shape = [jax.ShapeDtypeStruct((2 * kcount, width), F32)]
    return pl.pallas_call(
        functools.partial(phase_kernel, sizes, scale, paired),
        grid_spec=pltpu.PrefetchScalarGridSpec(
            num_scalar_prefetch=2,
            grid=(steps,),
            in_specs=[
                whole(3, 1, atoms),
                whole(atoms, width),
                pl.BlockSpec((3, kblock), kvec_map),
                whole(1, width),
                whole(width, width),
            ],
            out_specs=[
                pl.BlockSpec(memory_space=pltpu.HBM),
                pl.BlockSpec(memory_space=pltpu.VMEM),
                *out_specs,
            ],
            scratch_shapes=[
                pltpu.VMEM((atoms, 16), BF16),
                pltpu.VMEM((width, atoms), BF16),
                pltpu.VMEM((width, width), F32),
                pltpu.VMEM((width, width), F32),
                pltpu.VMEM((2, atoms, 2 * kblock), BF16),
                pltpu.SemaphoreType.DMA((2, 8)),
            ],
        ),
        out_shape=[
            pltpu.HBM((atoms, 2 * kcount), BF16),
            jax.ShapeDtypeStruct((atoms, width), BF16),
            *out_shape,
        ],
        compiler_params=pltpu.CompilerParams(vmem_limit_bytes=VMEM_LIMIT),
        name="phases",
    )(place, count, *in_hbm(pos.reshape(3, 1, atoms), feats, kvec, sigma.reshape(1, width), w_mix))


def select_kernel(send_ref, own_ref, *out_refs):
    faces, _, picks = send_ref.shape
    atoms, width = own_ref.shape
    rows = jnp.concatenate([send_ref[face] for face in range(faces)], axis=0).astype(F32)
    columns = jnp.concatenate([rows, jnp.zeros((8 - faces, picks), F32)], axis=0).T
    chunk = min(256, atoms)
    lane = lax.broadcasted_iota(jnp.int32, (picks, chunk), 1).astype(F32).astype(BF16)
    one, zero = jnp.ones((), BF16), jnp.zeros((), BF16)
    for face in range(faces):
        spread = jnp.broadcast_to(columns[:, face : face + 1], (picks, 128))
        total = jnp.zeros((picks, width), F32)
        for start in range(0, atoms, chunk):
            key = (spread - float(start)).astype(BF16)
            hot = jnp.where(jnp.concatenate([key] * (chunk // 128), axis=1) == lane, one, zero)
            total += jnp.dot(hot, own_ref[start : start + chunk, :], preferred_element_type=F32)
        if face < 4:
            out_refs[face][...] = total.astype(BF16)
        else:
            out_refs[4][face - 4] = total.astype(BF16)


def selected(send, own):
    width = own.shape[1]
    faces, _, picks = send.shape
    return pl.pallas_call(
        select_kernel,
        in_specs=[
            pl.BlockSpec((faces, 1, picks), lambda: (0, 0, 0)),
            pl.BlockSpec(memory_space=pltpu.VMEM),
        ],
        out_specs=[pl.BlockSpec(memory_space=pltpu.VMEM)] * 5,
        out_shape=[jax.ShapeDtypeStruct((picks, width), BF16)] * 4
        + [jax.ShapeDtypeStruct((2, picks, width), BF16)],
        compiler_params=pltpu.CompilerParams(vmem_limit_bytes=VMEM_LIMIT),
        name="selected",
    )(*in_hbm(send), own)


def total_kernel(parts_ref, out_ref):
    total = parts_ref[0].astype(F32)
    for part in range(1, parts_ref.shape[0]):
        total += parts_ref[part].astype(F32)
    total = total.astype(BF16)
    for part in range(parts_ref.shape[0]):
        out_ref[part] = total


def totals(parts):
    return pl.pallas_call(
        total_kernel,
        in_specs=[pl.BlockSpec(memory_space=pltpu.VMEM)],
        out_specs=pl.BlockSpec(memory_space=pltpu.VMEM),
        out_shape=jax.ShapeDtypeStruct(parts.shape, BF16),
        compiler_params=pltpu.CompilerParams(vmem_limit_bytes=4 << 20),
        name="totals",
    )(parts)


def prepare_kernel(low, nbr_ref, weight_ref, wmsg_ref, high_key, low_key, edge, wmsg_out):
    wmsg_out[...] = wmsg_ref[...]
    slots, atoms = nbr_ref.shape
    groups, lanes = high_key.shape
    stack = lambda ref: jnp.concatenate(
        [ref[:, i * groups : (i + 1) * groups].astype(F32) for i in range(8)], axis=0
    )
    picks = stack(nbr_ref)
    upper = jnp.floor(picks * (1.0 / low))
    low_key[...] = picks - upper * low
    place = lax.broadcasted_iota(jnp.int32, (lanes, groups), 0) // slots
    high_key[...] = (upper * 8.0 + place.astype(F32)).T
    edge[...] = stack(weight_ref).T


def prepared(low, nbr, weights, wmsg):
    slots, atoms = nbr.shape
    lanes, groups = 8 * slots, atoms // 8
    whole = lambda *shape: pl.BlockSpec(shape, lambda: (0,) * len(shape))
    return pl.pallas_call(
        functools.partial(prepare_kernel, low),
        in_specs=[whole(slots, atoms), whole(slots, atoms), whole(*wmsg.shape)],
        out_specs=[pl.BlockSpec(memory_space=pltpu.VMEM)] * 4,
        out_shape=[
            jax.ShapeDtypeStruct((groups, lanes), F32),
            jax.ShapeDtypeStruct((lanes, groups), F32),
            jax.ShapeDtypeStruct((groups, lanes), F32),
            jax.ShapeDtypeStruct(wmsg.shape, BF16),
        ],
        compiler_params=pltpu.CompilerParams(vmem_limit_bytes=VMEM_LIMIT),
        name="prepared",
    )(*in_hbm(nbr, weights, wmsg))


def build_adjacency(low, base, span, high_key, low_key, edge, store):
    groups, lanes = high_key.shape
    highs = store.highs
    high_iota = lax.broadcasted_iota(jnp.int32, (highs * 8, lanes), 0).astype(F32).astype(BF16)
    lane = lax.broadcasted_iota(jnp.int32, (lanes, 128), 1).astype(F32)
    low_iota = [(lane + 128.0 * part).astype(BF16) for part in range(low // 128)]
    tile = lambda x, n: jnp.concatenate([x] * (n // 16), axis=0)
    zero = jnp.zeros((), BF16)
    one = jnp.ones((), BF16)
    lane_tile = pl.multiple_of(base // 128 * 128, 128)
    lows = pltpu.roll(low_key[:, pl.ds(lane_tile, 128)], (128 - base % 128) % 128, 1)

    def group(number):
        row = pl.ds(base + number, 1)
        high = jnp.broadcast_to(high_key[row, :], (16, lanes)).astype(BF16)
        value = jnp.broadcast_to(edge[row, :], (16, lanes)).astype(BF16)
        left = jnp.where(tile(high, highs * 8) == high_iota, tile(value, highs * 8), zero)
        lower = jnp.broadcast_to(lows[:, number : number + 1], (lanes, 128)).astype(BF16)
        right = jnp.concatenate([jnp.where(lower == iota, one, zero) for iota in low_iota], axis=1)
        return jnp.dot(left, right, preferred_element_type=F32)

    for number in range(0, span, 2):
        one_group = group(number)
        next_group = group(number + 1)
        for upper in range(highs):
            rows = slice(upper * 8, upper * 8 + 8)
            block = jnp.concatenate([one_group[rows], next_group[rows]], axis=0).astype(BF16)
            store(number * 8, upper, block)


class Store:
    def __init__(self, own_ref, halo_ref, low):
        self.own_ref, self.halo_ref, self.low = own_ref, halo_ref, low
        self.split = own_ref.shape[1] // low
        self.highs = self.split + halo_ref.shape[1] // low

    def __call__(self, row, upper, block):
        ref = self.own_ref if upper < self.split else self.halo_ref
        upper -= 0 if upper < self.split else self.split
        ref[row : row + 16, upper * self.low : (upper + 1) * self.low] = block


def build_kernel(low, span, high_key, low_key, edge, own_ref, halo_adj, partial_ref, own_adj):
    store = Store(own_adj, halo_adj, low)
    build_adjacency(low, pl.program_id(0) * span, span, high_key, low_key, edge, store)
    partial_ref[...] = jnp.dot(own_adj[...], own_ref[...], preferred_element_type=F32)


def built(low, keys, own, halo_rows, here):
    atoms, width = own.shape
    span = min(64, here)
    vmem = pl.BlockSpec(memory_space=pltpu.VMEM)
    return pl.pallas_call(
        functools.partial(build_kernel, low, span),
        grid=(here // span,),
        in_specs=[vmem] * 4,
        out_specs=[
            pl.BlockSpec((8 * span, halo_rows), lambda b: (b, 0)),
            pl.BlockSpec((8 * span, width), lambda b: (b, 0)),
        ],
        out_shape=[pltpu.HBM((8 * here, halo_rows), BF16), jax.ShapeDtypeStruct((8 * here, width), F32)],
        scratch_shapes=[pltpu.VMEM((8 * span, atoms), BF16)],
        compiler_params=pltpu.CompilerParams(vmem_limit_bytes=VMEM_LIMIT),
        name="built",
    )(*keys, own)


def message_kernel(
    low, span, slots, early, count_ref, early_hbm, partial_ref, high_key, low_key, edge, own_ref, *refs
):
    halo_refs = [*refs[:4], refs[4].at[0], refs[4].at[1]]
    wmsg_ref, out_ref, early_adj, own_adj, halo_adj, msg_ref, sem = refs[-7:]
    atoms, width = own_ref.shape
    groups = high_key.shape[0]
    step = pl.program_id(0)
    steps = pl.num_programs(0)
    halo = jnp.concatenate([ref[...] for ref in halo_refs], axis=0)
    fetch = pltpu.make_async_copy(early_hbm, early_adj, sem)

    @pl.when(step == 0)
    def _():
        fetch.start()

    @pl.when(step == steps - early)
    def _():
        fetch.wait()

    @pl.when(step < steps - early)
    def _():
        store = Store(own_adj, halo_adj, low)
        build_adjacency(low, (step + early) * span, span, high_key, low_key, edge, store)
        summed = jnp.dot(own_adj[...], own_ref[...], preferred_element_type=F32)
        msg_ref[...] = summed + jnp.dot(halo_adj[...], halo, preferred_element_type=F32)

    @pl.when(step >= steps - early)
    def _():
        rows = pl.ds(pl.multiple_of((step + early - steps) * 8 * span, 8 * span), 8 * span)
        more = jnp.dot(early_adj[rows, :], halo, preferred_element_type=F32)
        msg_ref[...] = partial_ref[rows, :] + more

    message = (msg_ref[...] / math.sqrt(slots)).astype(BF16)
    hidden = jnp.dot(message, wmsg_ref[...], preferred_element_type=F32)
    msg_ref[...] = hidden / (1.0 + jnp.exp(-hidden))
    inside = pl.multiple_of(lax.rem(step + early, steps) * span, span)
    for i in range(8):
        start = pl.multiple_of(i * groups + inside, span)
        own = own_ref[pl.ds(start, span), :].astype(F32)
        gate = msg_ref[pl.ds(i, span, stride=8), :]
        atom = lax.broadcasted_iota(jnp.int32, (span, width), 0) + start
        out_ref[i] = jnp.where(atom < count_ref[0], own + gate, 0.0).astype(BF16)


def messages(low, count, early_adj, partial, keys, own, halos, wmsg, slots):
    groups = keys[0].shape[0]
    atoms, width = own.shape
    halo_rows = early_adj.shape[1]
    span = min(64, groups // 4)
    vmem = pl.BlockSpec(memory_space=pltpu.VMEM)
    arrays = [partial, *keys, own, *halos, wmsg]
    steps = groups // span
    early = early_adj.shape[0] // (8 * span)
    out = pl.pallas_call(
        functools.partial(message_kernel, low, span, slots, early),
        grid=(steps,),
        in_specs=[pl.BlockSpec(memory_space=pltpu.SMEM), pl.BlockSpec(memory_space=pltpu.HBM)]
        + [vmem] * len(arrays),
        out_specs=pl.BlockSpec((8, span, width), lambda b: (0, lax.rem(b + early, steps), 0)),
        out_shape=jax.ShapeDtypeStruct((8, groups, width), BF16),
        scratch_shapes=[
            pltpu.VMEM(early_adj.shape, BF16),
            pltpu.VMEM((8 * span, atoms), BF16),
            pltpu.VMEM((8 * span, halo_rows), BF16),
            pltpu.VMEM((8 * span, width), F32),
            pltpu.SemaphoreType.DMA,
        ],
        compiler_params=pltpu.CompilerParams(vmem_limit_bytes=VMEM_LIMIT),
        name="messages",
    )(count, *in_hbm(early_adj), *arrays)
    return out.reshape(atoms, width)


def back_kernel(scale, count_ref, table_hbm, *refs):
    *g_refs, out_hbm, table_ref, out_ref, sems, out_sems = refs
    atoms, width = out_ref.shape
    pieces = sems.shape[0]
    rows = atoms // pieces
    copies = []
    for piece in range(pieces):
        here = pl.ds(piece * rows, rows)
        copies.append(pltpu.make_async_copy(table_hbm.at[here], table_ref.at[here], sems.at[piece]))
        copies[-1].start()
    for piece in range(pieces):
        copies[piece].wait()
        here = slice(piece * rows, (piece + 1) * rows)
        back = jnp.zeros((rows, width), F32)
        start = 0
        for g_ref in g_refs:
            depth = g_ref.shape[0]
            back += jnp.dot(
                table_ref[here, start : start + depth], g_ref[...], preferred_element_type=F32
            )
            start += depth
        atom = lax.broadcasted_iota(jnp.int32, (rows, width), 0) + piece * rows
        out_ref[here, :] = jnp.where(atom < count_ref[0], back * scale, 0.0)
        here = pl.ds(piece * rows, rows)
        copies.append(pltpu.make_async_copy(out_ref.at[here], out_hbm.at[here], out_sems.at[piece]))
        copies[-1].start()
    for copy in copies[pieces:]:
        copy.wait()


def back(count, table, gs, scale):
    atoms, depth = table.shape
    width = gs[0].shape[1]
    vmem = pl.BlockSpec(memory_space=pltpu.VMEM)
    return pl.pallas_call(
        functools.partial(back_kernel, scale),
        in_specs=[
            pl.BlockSpec(memory_space=pltpu.SMEM),
            pl.BlockSpec(memory_space=pltpu.HBM),
            *[vmem for _ in gs],
        ],
        out_specs=pl.BlockSpec(memory_space=pltpu.HBM),
        out_shape=pltpu.HBM((atoms, width), F32),
        scratch_shapes=[
            pltpu.VMEM((atoms, depth), BF16),
            pltpu.VMEM((atoms, width), F32),
            pltpu.SemaphoreType.DMA((8,)),
            pltpu.SemaphoreType.DMA((8,)),
        ],
        compiler_params=pltpu.CompilerParams(vmem_limit_bytes=VMEM_LIMIT),
        name="back",
    )(count, *in_hbm(table), *gs)


def passed_along(value, axis, steps):
    size = lax.axis_size(axis)
    pairs = [(source, (source + steps) % size) for source in range(size)]
    return lax.ppermute(value, axis, pairs)


def shards(
    features, positions, counts, kvec, sigma, w_mix, neighbours, edge_weight, send_list, w_message
):
    atoms = features.shape[3]
    width = features.shape[4]
    kcount = kvec.shape[1]
    slots = neighbours.shape[3]
    feats = features.reshape(atoms, width)
    count = counts.reshape(1)
    sizes = [lax.axis_size(axis) for axis in ("gx", "gy", "gz")]
    plane = sizes[0] * sizes[1]
    devices = plane * sizes[2]
    place = jnp.stack([lax.axis_index(axis) for axis in ("gx", "gy", "gz")]).astype(jnp.int32)
    paired = sizes[2] == 2

    scale = 1.0 / math.sqrt(atoms * devices)
    table, own, *sums = phases(
        place, count, sizes, scale, positions.reshape(3, atoms), feats, kvec, sigma, w_mix
    )
    low = 256
    nbr, _ = lax.optimization_barrier((neighbours.reshape(slots, atoms), sums))
    *keys, wmsg = prepared(low, nbr, edge_weight.reshape(slots, atoms), w_message)
    if paired:
        mine = sums[1] + passed_along(sums[0], "gz", 1)
    else:
        parts = lax.all_to_all(sums[0], "gz", 0, 0, tiled=True)
        mine = jnp.sum(parts.reshape(sizes[2], -1, width), axis=0)
    part = mine.shape[0] // plane
    mine, keys, wmsg, send, own = lax.optimization_barrier((mine, keys, wmsg, send_list, own))

    received = lax.all_to_all(mine.reshape(plane, part, width), ("gx", "gy"), 0, 0, tiled=True)
    outgoing = selected(send.reshape(6, 1, -1), own)
    halos = [
        passed_along(outgoing[2 * number + side], axis, 1 - 2 * side)
        for number, axis in enumerate(("gx", "gy"))
        for side in range(2)
    ]
    if paired:
        halos.append(passed_along(outgoing[4], "gz", 1))
    else:
        halos.append(jnp.stack([passed_along(outgoing[4][side], "gz", 1 - 2 * side) for side in range(2)]))
    adjacency = built(low, keys, own, send.size, atoms // 8 // 4 * EARLY)
    received, halos, adjacency = lax.optimization_barrier((received, halos, adjacency))

    shares = totals(received)
    g = lax.all_to_all(shares, ("gx", "gy"), 0, 0, tiled=True).reshape(plane * part, width)
    halos, _ = lax.optimization_barrier((halos, shares))
    updated = messages(low, count, *adjacency, keys, own, halos, wmsg, slots)
    g, updated = lax.optimization_barrier((g, updated))
    if paired:
        gs = [passed_along(g, "gz", 1), g]
    else:
        gs = [lax.all_gather(g, "gz", tiled=True)]
    long_range = back(count, table, gs, 2.0 / math.sqrt(kcount))
    return (updated.reshape(1, 1, 1, atoms, width), long_range.reshape(1, 1, 1, atoms, width))


def solution(mesh):
    split = P("gx", "gy", "gz", None, None)
    placed = (split, split, P("gx", "gy", "gz"), P(), P(), P(), split, split, split, P())
    return jax.shard_map(
        shards, mesh=mesh, in_specs=placed, out_specs=(split, split), check_vma=False
    )
```

```python
import functools
import math

import jax
import jax.numpy as jnp
import numpy as np
from jax import lax
from jax.experimental import pallas as pl
from jax.experimental.pallas import tpu as pltpu
from jax.sharding import PartitionSpec as P

F32 = jnp.float32
BF16 = jnp.bfloat16
VMEM_LIMIT = 22 << 20
EARLY = 2


def half_turn_series():
    angle = np.cos((np.arange(400) + 0.5) * np.pi / 800)
    r = 0.5 * angle
    u = r * r
    root = math.sqrt(2.0)
    even = np.polynomial.chebyshev.Chebyshev.fit(u, root * np.cos(np.pi * r), 4, domain=[0, 0.25])
    odd = np.polynomial.chebyshev.Chebyshev.fit(u, root * np.sin(np.pi * r) / r, 4, domain=[0, 0.25])
    take = lambda fit: [float(v) for v in fit.convert(kind=np.polynomial.Polynomial).coef]
    return take(even), take(odd)


EVEN, ODD = half_turn_series()


def in_hbm(*values):
    return [pltpu.with_memory_space_constraint(value, pltpu.HBM) for value in values]


def horner(coefs, u):
    total = coefs[-1] * u + coefs[-2]
    for coef in coefs[-3::-1]:
        total = total * u + coef
    return total


def phase_kernel(
    sizes,
    scale,
    paired,
    place_ref,
    count_ref,
    pos_ref,
    feat_ref,
    kvec_ref,
    sigma_ref,
    mix_ref,
    table_ref,
    live_ref,
    *refs,
):
    out_refs = refs[: 1 + paired]
    frac_ref, own_ref, mix_turned, decay_ref, block_ref, sems = refs[1 + paired :]
    atoms, width = feat_ref.shape
    kblock = kvec_ref.shape[1]
    step = pl.program_id(0)

    @pl.when(step == 0)
    def _():
        rows = []
        for axis in range(3):
            frac = (place_ref[axis].astype(F32) + pos_ref[axis]) / sizes[axis]
            high = frac.astype(BF16).astype(F32)
            middle = (frac - high).astype(BF16).astype(F32)
            rows += [high, middle, frac - high - middle]
        stacked = jnp.concatenate(rows + [jnp.zeros((16 - len(rows), atoms), F32)], axis=0)
        frac_ref[...] = stacked.T.astype(BF16)
        atom = lax.broadcasted_iota(jnp.int32, (atoms, width), 0)
        own = jnp.where(atom < count_ref[0], feat_ref[...].astype(F32), 0.0)
        own_ref[...] = own.T.astype(BF16)
        live_ref[...] = own.astype(BF16)
        mix_turned[...] = mix_ref[...].T
        decay_ref[...] = jnp.broadcast_to(-sigma_ref[...], (width, width)).T

    kvec = kvec_ref[...].astype(F32)
    weights = jnp.concatenate(
        [kvec[axis : axis + 1, :] for axis in range(3) for _ in range(3)]
        + [jnp.zeros((7, kblock), F32)],
        axis=0,
    ).astype(BF16)
    chunk = atoms // sems.shape[1]
    slot = lax.rem(step, 2)

    def store(number, which, column):
        rows = pl.ds(number * chunk, chunk)
        columns = pl.ds(pl.multiple_of(column * 2 * kblock, 2 * kblock), 2 * kblock)
        return pltpu.make_async_copy(
            block_ref.at[which, rows], table_ref.at[rows, columns], sems.at[which, number]
        )

    @pl.when(step >= 2)
    def _():
        for number in range(atoms // chunk):
            store(number, slot, step - 2).wait()

    for start in range(0, atoms, chunk):
        rows = slice(start, start + chunk)
        theta = jnp.dot(frac_ref[rows, :], weights, preferred_element_type=F32)
        r = theta - jnp.round(theta)
        u = r * r
        even = horner(EVEN, u)
        odd = horner(ODD, u) * r
        cosine = (1.0 - odd * odd).astype(BF16)
        sine = (even * odd).astype(BF16)
        block_ref[slot, rows, :kblock] = cosine
        block_ref[slot, rows, kblock:] = sine
        store(start // chunk, slot, step).start()

    sums = jnp.dot(own_ref[...], block_ref[slot], preferred_element_type=F32)
    ksq = jnp.sum(kvec * kvec, axis=0, keepdims=True)
    decay = jnp.exp(decay_ref[:, :1] * ksq)
    mixed = jnp.dot(
        mix_turned[...], sums * scale, precision=lax.Precision.HIGHEST, preferred_element_type=F32
    )
    result = (mixed * jnp.concatenate([decay, decay], axis=1)).T
    if paired:
        half = pl.num_programs(0) // 2

        @pl.when(step < half)
        def _():
            out_refs[0][...] = result

        @pl.when(step >= half)
        def _():
            out_refs[1][...] = result
    else:
        out_refs[0][...] = result

    @pl.when(step == pl.num_programs(0) - 1)
    def _():
        for number in range(atoms // chunk):
            store(number, 1 - slot, step - 1).wait()
            store(number, slot, step).wait()


def phases(place, count, sizes, scale, pos, feats, kvec, sigma, w_mix):
    atoms, width = feats.shape
    kcount = kvec.shape[1]
    kblock = 512 if kcount % 1024 == 0 else 128
    steps = kcount // kblock
    half = steps // 2
    paired = sizes[2] == 2
    whole = lambda *shape: pl.BlockSpec(shape, lambda b, *_: (0,) * len(shape))

    def kvec_map(b, place_ref, count_ref):
        return (0, lax.rem(b + (1 - place_ref[2]) * half, steps) if paired else b)

    if paired:
        out_specs = [
            pl.BlockSpec((2 * kblock, width), lambda b, *_: (jnp.minimum(b, half - 1), 0)),
            pl.BlockSpec((2 * kblock, width), lambda b, *_: (jnp.maximum(b - half, 0), 0)),
        ]
        out_shape = [jax.ShapeDtypeStruct((kcount, width), F32)] * 2
    else:
        out_specs = [pl.BlockSpec((2 * kblock, width), lambda b, *_: (b, 0))]
        out_shape = [jax.ShapeDtypeStruct((2 * kcount, width), F32)]
    return pl.pallas_call(
        functools.partial(phase_kernel, sizes, scale, paired),
        grid_spec=pltpu.PrefetchScalarGridSpec(
            num_scalar_prefetch=2,
            grid=(steps,),
            in_specs=[
                whole(3, 1, atoms),
                whole(atoms, width),
                pl.BlockSpec((3, kblock), kvec_map),
                whole(1, width),
                whole(width, width),
            ],
            out_specs=[
                pl.BlockSpec(memory_space=pltpu.HBM),
                pl.BlockSpec(memory_space=pltpu.VMEM),
                *out_specs,
            ],
            scratch_shapes=[
                pltpu.VMEM((atoms, 16), BF16),
                pltpu.VMEM((width, atoms), BF16),
                pltpu.VMEM((width, width), F32),
                pltpu.VMEM((width, width), F32),
                pltpu.VMEM((2, atoms, 2 * kblock), BF16),
                pltpu.SemaphoreType.DMA((2, 8)),
            ],
        ),
        out_shape=[
            pltpu.HBM((atoms, 2 * kcount), BF16),
            jax.ShapeDtypeStruct((atoms, width), BF16),
            *out_shape,
        ],
        compiler_params=pltpu.CompilerParams(vmem_limit_bytes=VMEM_LIMIT),
        name="phases",
    )(place, count, *in_hbm(pos.reshape(3, 1, atoms), feats, kvec, sigma.reshape(1, width), w_mix))


def select_kernel(send_ref, own_ref, *out_refs):
    faces, _, picks = send_ref.shape
    atoms, width = own_ref.shape
    rows = jnp.concatenate([send_ref[face] for face in range(faces)], axis=0).astype(F32)
    columns = jnp.concatenate([rows, jnp.zeros((8 - faces, picks), F32)], axis=0).T
    chunk = min(256, atoms)
    lane = lax.broadcasted_iota(jnp.int32, (picks, chunk), 1).astype(F32).astype(BF16)
    one, zero = jnp.ones((), BF16), jnp.zeros((), BF16)
    for face in range(faces):
        spread = jnp.broadcast_to(columns[:, face : face + 1], (picks, 128))
        total = jnp.zeros((picks, width), F32)
        for start in range(0, atoms, chunk):
            key = (spread - float(start)).astype(BF16)
            hot = jnp.where(jnp.concatenate([key] * (chunk // 128), axis=1) == lane, one, zero)
            total += jnp.dot(hot, own_ref[start : start + chunk, :], preferred_element_type=F32)
        if face < 4:
            out_refs[face][...] = total.astype(BF16)
        else:
            out_refs[4][face - 4] = total.astype(BF16)


def selected(send, own):
    width = own.shape[1]
    faces, _, picks = send.shape
    return pl.pallas_call(
        select_kernel,
        in_specs=[
            pl.BlockSpec((faces, 1, picks), lambda: (0, 0, 0)),
            pl.BlockSpec(memory_space=pltpu.VMEM),
        ],
        out_specs=[pl.BlockSpec(memory_space=pltpu.VMEM)] * 5,
        out_shape=[jax.ShapeDtypeStruct((picks, width), BF16)] * 4
        + [jax.ShapeDtypeStruct((2, picks, width), BF16)],
        compiler_params=pltpu.CompilerParams(vmem_limit_bytes=VMEM_LIMIT),
        name="selected",
    )(*in_hbm(send), own)


def total_kernel(parts_ref, out_ref):
    total = parts_ref[0].astype(F32)
    for part in range(1, parts_ref.shape[0]):
        total += parts_ref[part].astype(F32)
    total = total.astype(BF16)
    for part in range(parts_ref.shape[0]):
        out_ref[part] = total


def totals(parts):
    return pl.pallas_call(
        total_kernel,
        in_specs=[pl.BlockSpec(memory_space=pltpu.VMEM)],
        out_specs=pl.BlockSpec(memory_space=pltpu.VMEM),
        out_shape=jax.ShapeDtypeStruct(parts.shape, BF16),
        compiler_params=pltpu.CompilerParams(vmem_limit_bytes=4 << 20),
        name="totals",
    )(parts)


def prepare_kernel(low, nbr_ref, weight_ref, wmsg_ref, high_key, low_key, edge, wmsg_out):
    wmsg_out[...] = wmsg_ref[...]
    slots, atoms = nbr_ref.shape
    groups, lanes = high_key.shape
    stack = lambda ref: jnp.concatenate(
        [ref[:, i * groups : (i + 1) * groups].astype(F32) for i in range(8)], axis=0
    )
    picks = stack(nbr_ref)
    upper = jnp.floor(picks * (1.0 / low))
    low_key[...] = picks - upper * low
    place = lax.broadcasted_iota(jnp.int32, (lanes, groups), 0) // slots
    high_key[...] = (upper * 8.0 + place.astype(F32)).T
    edge[...] = stack(weight_ref).T


def prepared(low, nbr, weights, wmsg):
    slots, atoms = nbr.shape
    lanes, groups = 8 * slots, atoms // 8
    whole = lambda *shape: pl.BlockSpec(shape, lambda: (0,) * len(shape))
    return pl.pallas_call(
        functools.partial(prepare_kernel, low),
        in_specs=[whole(slots, atoms), whole(slots, atoms), whole(*wmsg.shape)],
        out_specs=[pl.BlockSpec(memory_space=pltpu.VMEM)] * 4,
        out_shape=[
            jax.ShapeDtypeStruct((groups, lanes), F32),
            jax.ShapeDtypeStruct((lanes, groups), F32),
            jax.ShapeDtypeStruct((groups, lanes), F32),
            jax.ShapeDtypeStruct(wmsg.shape, BF16),
        ],
        compiler_params=pltpu.CompilerParams(vmem_limit_bytes=VMEM_LIMIT),
        name="prepared",
    )(*in_hbm(nbr, weights, wmsg))


def build_adjacency(low, base, span, high_key, low_key, edge, store):
    groups, lanes = high_key.shape
    highs = store.highs
    high_iota = lax.broadcasted_iota(jnp.int32, (highs * 8, lanes), 0).astype(F32).astype(BF16)
    lane = lax.broadcasted_iota(jnp.int32, (lanes, 128), 1).astype(F32)
    low_iota = [(lane + 128.0 * part).astype(BF16) for part in range(low // 128)]
    tile = lambda x, n: jnp.concatenate([x] * (n // 16), axis=0)
    zero = jnp.zeros((), BF16)
    one = jnp.ones((), BF16)
    lane_tile = pl.multiple_of(base // 128 * 128, 128)
    lows = pltpu.roll(low_key[:, pl.ds(lane_tile, 128)], (128 - base % 128) % 128, 1)

    def group(number):
        row = pl.ds(base + number, 1)
        high = jnp.broadcast_to(high_key[row, :], (16, lanes)).astype(BF16)
        value = jnp.broadcast_to(edge[row, :], (16, lanes)).astype(BF16)
        left = jnp.where(tile(high, highs * 8) == high_iota, tile(value, highs * 8), zero)
        lower = jnp.broadcast_to(lows[:, number : number + 1], (lanes, 128)).astype(BF16)
        right = jnp.concatenate([jnp.where(lower == iota, one, zero) for iota in low_iota], axis=1)
        return jnp.dot(left, right, preferred_element_type=F32)

    for number in range(0, span, 2):
        one_group = group(number)
        next_group = group(number + 1)
        for upper in range(highs):
            rows = slice(upper * 8, upper * 8 + 8)
            block = jnp.concatenate([one_group[rows], next_group[rows]], axis=0).astype(BF16)
            store(number * 8, upper, block)


class Store:
    def __init__(self, own_ref, halo_ref, low):
        self.own_ref, self.halo_ref, self.low = own_ref, halo_ref, low
        self.split = own_ref.shape[1] // low
        self.highs = self.split + halo_ref.shape[1] // low

    def __call__(self, row, upper, block):
        ref = self.own_ref if upper < self.split else self.halo_ref
        upper -= 0 if upper < self.split else self.split
        ref[row : row + 16, upper * self.low : (upper + 1) * self.low] = block


def build_kernel(low, span, high_key, low_key, edge, own_ref, halo_adj, partial_ref, own_adj):
    store = Store(own_adj, halo_adj, low)
    build_adjacency(low, pl.program_id(0) * span, span, high_key, low_key, edge, store)
    partial_ref[...] = jnp.dot(own_adj[...], own_ref[...], preferred_element_type=F32)


def built(low, keys, own, halo_rows, here):
    atoms, width = own.shape
    span = min(64, here)
    vmem = pl.BlockSpec(memory_space=pltpu.VMEM)
    return pl.pallas_call(
        functools.partial(build_kernel, low, span),
        grid=(here // span,),
        in_specs=[vmem] * 4,
        out_specs=[
            pl.BlockSpec((8 * span, halo_rows), lambda b: (b, 0)),
            pl.BlockSpec((8 * span, width), lambda b: (b, 0)),
        ],
        out_shape=[pltpu.HBM((8 * here, halo_rows), BF16), jax.ShapeDtypeStruct((8 * here, width), F32)],
        scratch_shapes=[pltpu.VMEM((8 * span, atoms), BF16)],
        compiler_params=pltpu.CompilerParams(vmem_limit_bytes=VMEM_LIMIT),
        name="built",
    )(*keys, own)


def message_kernel(
    low, span, slots, early, count_ref, early_hbm, partial_ref, high_key, low_key, edge, own_ref, *refs
):
    halo_refs = [*refs[:4], refs[4].at[0], refs[4].at[1]]
    wmsg_ref, out_ref, early_adj, own_adj, halo_adj, msg_ref, sem = refs[-7:]
    atoms, width = own_ref.shape
    groups = high_key.shape[0]
    step = pl.program_id(0)
    steps = pl.num_programs(0)
    halo = jnp.concatenate([ref[...] for ref in halo_refs], axis=0)
    fetch = pltpu.make_async_copy(early_hbm, early_adj, sem)

    @pl.when(step == 0)
    def _():
        fetch.start()

    @pl.when(step == steps - early)
    def _():
        fetch.wait()

    @pl.when(step < steps - early)
    def _():
        store = Store(own_adj, halo_adj, low)
        build_adjacency(low, (step + early) * span, span, high_key, low_key, edge, store)
        summed = jnp.dot(own_adj[...], own_ref[...], preferred_element_type=F32)
        msg_ref[...] = summed + jnp.dot(halo_adj[...], halo, preferred_element_type=F32)

    @pl.when(step >= steps - early)
    def _():
        rows = pl.ds(pl.multiple_of((step + early - steps) * 8 * span, 8 * span), 8 * span)
        more = jnp.dot(early_adj[rows, :], halo, preferred_element_type=F32)
        msg_ref[...] = partial_ref[rows, :] + more

    message = (msg_ref[...] / math.sqrt(slots)).astype(BF16)
    hidden = jnp.dot(message, wmsg_ref[...], preferred_element_type=F32)
    msg_ref[...] = hidden / (1.0 + jnp.exp(-hidden))
    inside = pl.multiple_of(lax.rem(step + early, steps) * span, span)
    for i in range(8):
        start = pl.multiple_of(i * groups + inside, span)
        own = own_ref[pl.ds(start, span), :].astype(F32)
        gate = msg_ref[pl.ds(i, span, stride=8), :]
        atom = lax.broadcasted_iota(jnp.int32, (span, width), 0) + start
        out_ref[i] = jnp.where(atom < count_ref[0], own + gate, 0.0).astype(BF16)


def messages(low, count, early_adj, partial, keys, own, halos, wmsg, slots):
    groups = keys[0].shape[0]
    atoms, width = own.shape
    halo_rows = early_adj.shape[1]
    span = min(128, groups // 2)
    vmem = pl.BlockSpec(memory_space=pltpu.VMEM)
    arrays = [partial, *keys, own, *halos, wmsg]
    steps = groups // span
    early = early_adj.shape[0] // (8 * span)
    out = pl.pallas_call(
        functools.partial(message_kernel, low, span, slots, early),
        grid=(steps,),
        in_specs=[pl.BlockSpec(memory_space=pltpu.SMEM), pl.BlockSpec(memory_space=pltpu.HBM)]
        + [vmem] * len(arrays),
        out_specs=pl.BlockSpec((8, span, width), lambda b: (0, lax.rem(b + early, steps), 0)),
        out_shape=jax.ShapeDtypeStruct((8, groups, width), BF16),
        scratch_shapes=[
            pltpu.VMEM(early_adj.shape, BF16),
            pltpu.VMEM((8 * span, atoms), BF16),
            pltpu.VMEM((8 * span, halo_rows), BF16),
            pltpu.VMEM((8 * span, width), F32),
            pltpu.SemaphoreType.DMA,
        ],
        compiler_params=pltpu.CompilerParams(vmem_limit_bytes=VMEM_LIMIT),
        name="messages",
    )(count, *in_hbm(early_adj), *arrays)
    return out.reshape(atoms, width)


def back_kernel(scale, count_ref, table_hbm, *refs):
    *g_refs, out_hbm, table_ref, out_ref, sems, out_sems = refs
    atoms, width = out_ref.shape
    pieces = sems.shape[0]
    rows = atoms // pieces
    copies = []
    for piece in range(pieces):
        here = pl.ds(piece * rows, rows)
        copies.append(pltpu.make_async_copy(table_hbm.at[here], table_ref.at[here], sems.at[piece]))
        copies[-1].start()
    for piece in range(pieces):
        copies[piece].wait()
        here = slice(piece * rows, (piece + 1) * rows)
        back = jnp.zeros((rows, width), F32)
        start = 0
        for g_ref in g_refs:
            depth = g_ref.shape[0]
            back += jnp.dot(
                table_ref[here, start : start + depth], g_ref[...], preferred_element_type=F32
            )
            start += depth
        atom = lax.broadcasted_iota(jnp.int32, (rows, width), 0) + piece * rows
        out_ref[here, :] = jnp.where(atom < count_ref[0], back * scale, 0.0)
        here = pl.ds(piece * rows, rows)
        copies.append(pltpu.make_async_copy(out_ref.at[here], out_hbm.at[here], out_sems.at[piece]))
        copies[-1].start()
    for copy in copies[pieces:]:
        copy.wait()


def back(count, table, gs, scale):
    atoms, depth = table.shape
    width = gs[0].shape[1]
    vmem = pl.BlockSpec(memory_space=pltpu.VMEM)
    return pl.pallas_call(
        functools.partial(back_kernel, scale),
        in_specs=[
            pl.BlockSpec(memory_space=pltpu.SMEM),
            pl.BlockSpec(memory_space=pltpu.HBM),
            *[vmem for _ in gs],
        ],
        out_specs=pl.BlockSpec(memory_space=pltpu.HBM),
        out_shape=pltpu.HBM((atoms, width), F32),
        scratch_shapes=[
            pltpu.VMEM((atoms, depth), BF16),
            pltpu.VMEM((atoms, width), F32),
            pltpu.SemaphoreType.DMA((8,)),
            pltpu.SemaphoreType.DMA((8,)),
        ],
        compiler_params=pltpu.CompilerParams(vmem_limit_bytes=VMEM_LIMIT),
        name="back",
    )(count, *in_hbm(table), *gs)


def passed_along(value, axis, steps):
    size = lax.axis_size(axis)
    pairs = [(source, (source + steps) % size) for source in range(size)]
    return lax.ppermute(value, axis, pairs)


def shards(
    features, positions, counts, kvec, sigma, w_mix, neighbours, edge_weight, send_list, w_message
):
    atoms = features.shape[3]
    width = features.shape[4]
    kcount = kvec.shape[1]
    slots = neighbours.shape[3]
    feats = features.reshape(atoms, width)
    count = counts.reshape(1)
    sizes = [lax.axis_size(axis) for axis in ("gx", "gy", "gz")]
    plane = sizes[0] * sizes[1]
    devices = plane * sizes[2]
    place = jnp.stack([lax.axis_index(axis) for axis in ("gx", "gy", "gz")]).astype(jnp.int32)
    paired = sizes[2] == 2

    scale = 1.0 / math.sqrt(atoms * devices)
    table, own, *sums = phases(
        place, count, sizes, scale, positions.reshape(3, atoms), feats, kvec, sigma, w_mix
    )
    low = 256
    nbr, _ = lax.optimization_barrier((neighbours.reshape(slots, atoms), sums))
    *keys, wmsg = prepared(low, nbr, edge_weight.reshape(slots, atoms), w_message)
    if paired:
        mine = sums[1] + passed_along(sums[0], "gz", 1)
    else:
        parts = lax.all_to_all(sums[0], "gz", 0, 0, tiled=True)
        mine = jnp.sum(parts.reshape(sizes[2], -1, width), axis=0)
    part = mine.shape[0] // plane
    mine, keys, wmsg, send, own = lax.optimization_barrier((mine, keys, wmsg, send_list, own))

    received = lax.all_to_all(mine.reshape(plane, part, width), ("gx", "gy"), 0, 0, tiled=True)
    outgoing = selected(send.reshape(6, 1, -1), own)
    halos = [
        passed_along(outgoing[2 * number + side], axis, 1 - 2 * side)
        for number, axis in enumerate(("gx", "gy"))
        for side in range(2)
    ]
    if paired:
        halos.append(passed_along(outgoing[4], "gz", 1))
    else:
        halos.append(jnp.stack([passed_along(outgoing[4][side], "gz", 1 - 2 * side) for side in range(2)]))
    adjacency = built(low, keys, own, send.size, atoms // 8 // 4 * EARLY)
    received, halos, adjacency = lax.optimization_barrier((received, halos, adjacency))

    shares = totals(received)
    g = lax.all_to_all(shares, ("gx", "gy"), 0, 0, tiled=True).reshape(plane * part, width)
    halos, _ = lax.optimization_barrier((halos, shares))
    updated = messages(low, count, *adjacency, keys, own, halos, wmsg, slots)
    g, updated = lax.optimization_barrier((g, updated))
    if paired:
        gs = [passed_along(g, "gz", 1), g]
    else:
        gs = [lax.all_gather(g, "gz", tiled=True)]
    long_range = back(count, table, gs, 2.0 / math.sqrt(kcount))
    return (updated.reshape(1, 1, 1, atoms, width), long_range.reshape(1, 1, 1, atoms, width))


def solution(mesh):
    split = P("gx", "gy", "gz", None, None)
    placed = (split, split, P("gx", "gy", "gz"), P(), P(), P(), split, split, split, P())
    return jax.shard_map(
        shards, mesh=mesh, in_specs=placed, out_specs=(split, split), check_vma=False
    )
```
